32 devices in a mesh: dp: 8 (over z, core), seq: 4 (over y, x).
Axes of the slice: x: 2, y: 2, z: 4, core: 2. Of those that a mesh axis runs over, the one named last changes fastest.
Arguments:
- tokens: int32 [8, 65536], P('dp', 'seq'), may hold values from 0 to 4
- stem_weight: bfloat16 [60, 768], replicated, may hold values from -1.5 to 1.5
- stem_bias: float32 [768], replicated, may hold values from -3 to 3
- conv_gain: float32 [768], replicated, may hold values from 0.1 to 1.9
- conv_weight: bfloat16 [5, 768, 1536], P(None, 'dp'), may hold values from -0.09375 to 0.09375
- conv_bias: float32 [1536], replicated, may hold values from -3 to 3
- attn_gain: float32 [1536], replicated, may hold values from 0.1 to 1.9
- w_query: bfloat16 [1536, 1024], P('dp'), may hold values from -7 to 7
- w_key: bfloat16 [1536, 128], P('dp'), may hold values from -0.15625 to 0.15625
- w_value: bfloat16 [1536, 192], P('dp'), may hold values from -0.15625 to 0.15625
- w_out: bfloat16 [1536, 1536], P('dp'), may hold values from -0.4375 to 0.4375
Outputs:
- features: bfloat16 [8, 512, 1536], P('dp', 'seq')
The draws below stay inside these ranges and needn't reach their ends.
Inputs may be any that keep to these rules, and one draw needn't show every extreme that they name: `tokens`: 0 is an unknown base; 1 to 4 are A, C, G, T.
All inputs are finite; a program needn't handle non-finite values.
Results may differ from the reference program's by a relative error of at most 0.009.
The reference program's roundings to bfloat16 on the way count: a program that leaves them out, or rounds other values in their place, can miss the bound.
Values may be sent and summed in bfloat16 or wider, within the bound.
A program may use at most 192 MiB of HBM per device.

```python
import math
import jax
import jax.numpy as jnp
from jax import lax

D_STEM = 768
D = 1536
HEADS = 8
HEAD_K = 128
HEAD_V = 192
KW_STEM = 15
KW = 5
POOL_A = 8
POOL_B = 16
STEM_IN = 60
LENGTH = 65536
POSITIONS = 512
WINDOWS = 8


def draw_w_query(key, part):
    normal_part = jnp.clip(jax.random.normal(key, (D, HEADS * HEAD_K), jnp.float32), -4.0, 4.0) * (1.0 / math.sqrt(D))
    return normal_part.astype(jnp.bfloat16)


def with_ends(drawn, rng, smallest, largest):
    extent = drawn.shape
    spot = [jax.random.randint(jax.random.fold_in(rng, axis), (), 0, extent[axis]) for axis in range(len(extent))]
    drawn = drawn.at[tuple(spot)].set(smallest)
    longest = extent.index(max(extent))
    spot[longest] = (spot[longest] + 1) % extent[longest]
    return drawn.at[tuple(spot)].set(largest)


def level_of(key, extent, split, least, high):
    def one(dim, blocks):
        draws = jax.random.uniform(jax.random.fold_in(jax.random.fold_in(key, 6), dim), (blocks,), jnp.float32, least / len(split), high / len(split))
        return jnp.repeat(jnp.exp(draws), extent[dim] // blocks).reshape((-1,) + (1,) * (len(extent) - dim - 1))

    loudness = one(*split[0])
    for cut in split[1:]:
        loudness = loudness * one(*cut)
    return loudness


def normal_values(own_key, shape, spread, most, cuts=(), held_as=jnp.bfloat16):
    level = level_of(own_key, shape, cuts, -0.22, 0.18) if cuts else 1.0
    array = jax.random.normal(own_key, shape, jnp.float32) * spread * level
    return jnp.minimum(jnp.maximum(array, -most), most).astype(held_as)


def setup_inputs(seed: int = 0) -> dict:
    streams_of = jax.random.split(jax.random.key(seed), 12)
    tokens = with_ends(jax.random.randint(streams_of[0], (WINDOWS, LENGTH), 0, 5), jax.random.fold_in(streams_of[0], 1), 0, 4).astype(jnp.int32)
    stem_weight = normal_values(streams_of[1], (STEM_IN, D_STEM), KW_STEM ** -0.5, 1.5)
    stem_bias = normal_values(streams_of[2], (D_STEM,), 0.5, 3.0, (), jnp.float32)
    conv_gain = jnp.clip(1.0 + 0.18 * jax.random.normal(streams_of[3], (D_STEM,), jnp.float32), 0.1, 1.9)
    conv_weight = normal_values(streams_of[4], (KW, D_STEM, D), (KW * D_STEM) ** -0.5, 0.09375, ((1, 8),))
    conv_bias = normal_values(streams_of[5], (D,), 0.5, 3.0, (), jnp.float32)
    attn_gain = jnp.clip(1.0 + 0.18 * jax.random.normal(streams_of[6], (D,), jnp.float32), 0.1, 1.9)
    w_query = draw_w_query(jax.random.fold_in(streams_of[11], 71), 0)
    w_key = normal_values(streams_of[8], (D, HEAD_K), D ** -0.5, 0.15625, ((0, 8),))
    w_value = normal_values(streams_of[9], (D, HEAD_V), D ** -0.5, 0.15625, ((0, 8),))
    w_out = normal_values(streams_of[10], (HEADS * HEAD_V, D), HEAD_V ** -0.5, 0.4375, ((0, 8),))
    return {"tokens": tokens, "stem_weight": stem_weight, "stem_bias": stem_bias, "conv_gain": conv_gain, "conv_weight": conv_weight, "conv_bias": conv_bias, "attn_gain": attn_gain, "w_query": w_query, "w_key": w_key, "w_value": w_value, "w_out": w_out}


epsilon = 1e-06

def stem_pool(padded_tokens, count, stem_weight, stem_bias):
    columns = jnp.stack([padded_tokens[offset:offset + count] for offset in range(KW_STEM)], axis=1)
    codes = jnp.arange(1, 5, dtype=jnp.int32)
    onehot = (columns[:, :, None] == codes).astype(jnp.bfloat16).reshape(count, KW_STEM * 4)
    block_len = min(count, 1024)
    onehot = onehot.reshape(count // block_len, block_len, KW_STEM * 4)

    def one_block(inputs):
        stem_rows = jnp.dot(inputs, stem_weight, preferred_element_type=jnp.float32) + stem_bias
        return jax.nn.gelu(lax.optimization_barrier(jnp.max(stem_rows.reshape(block_len // POOL_A, POOL_A, -1), axis=1)))
    return lax.map(one_block, onehot).reshape(count // POOL_A, -1).astype(jnp.bfloat16)

def rms_scale(values, gain):
    return values * lax.rsqrt(lax.optimization_barrier(jnp.mean(values * values, axis=-1, keepdims=True)) + epsilon) * gain

def rotate(values, angles):
    half_dim = values.shape[-1] // 2
    first = values[..., :half_dim]
    second = values[..., half_dim:]
    cosine = jnp.cos(angles)
    sine = jnp.sin(angles)
    return jnp.concatenate([first * cosine - second * sine, second * cosine + first * sine], axis=-1)

def reference(tokens, stem_weight, stem_bias, conv_gain, conv_weight, conv_bias, attn_gain, w_query, w_key, w_value, w_out):
    reach = KW_STEM // 2
    edge_rows = KW // 2

    def one_window(window_tokens):
        padded_tokens = jnp.pad(window_tokens, (reach, reach))
        pooled = stem_pool(padded_tokens, LENGTH, stem_weight, stem_bias)
        normed = rms_scale(pooled.astype(jnp.float32), conv_gain).astype(jnp.bfloat16)
        row_count = LENGTH // POOL_A
        padded_rows = jnp.pad(normed, ((edge_rows, edge_rows), (0, 0)))
        conv_sum = jnp.zeros((row_count, D), jnp.float32) + conv_bias
        for offset in range(KW):
            conv_sum = conv_sum + jnp.dot(padded_rows[offset:offset + row_count], conv_weight[offset], preferred_element_type=jnp.float32)
        coarse = lax.optimization_barrier(jnp.max(jax.nn.gelu(conv_sum).reshape(row_count // POOL_B, POOL_B, D), axis=1)).astype(jnp.bfloat16)
        residual = coarse.astype(jnp.float32)
        hidden = rms_scale(residual, attn_gain).astype(jnp.bfloat16)
        query = jnp.dot(hidden, w_query, preferred_element_type=jnp.float32).reshape(POSITIONS, HEADS, HEAD_K)
        keys = jnp.dot(hidden, w_key, preferred_element_type=jnp.float32)
        values = jnp.dot(hidden, w_value, preferred_element_type=jnp.float32).astype(jnp.bfloat16)
        half_dim = HEAD_K // 2
        freqs = 10000.0 ** (-jnp.arange(half_dim, dtype=jnp.float32) / half_dim)
        angles = jnp.arange(POSITIONS, dtype=jnp.int32).astype(jnp.float32)[:, None] * freqs[None, :]
        query = rotate(query, angles[:, None, :]).astype(jnp.bfloat16)
        keys = rotate(keys, angles).astype(jnp.bfloat16)
        scores = jnp.einsum('rhd,kd->hrk', query.astype(jnp.float32), keys.astype(jnp.float32)) * HEAD_K ** (-0.5)
        weights = jax.nn.softmax(scores, axis=-1).astype(jnp.bfloat16)
        mixed = jnp.einsum('hrk,kd->rhd', weights.astype(jnp.float32), values.astype(jnp.float32)).astype(jnp.bfloat16)
        mixed = mixed.reshape(POSITIONS, HEADS * HEAD_V)
        return (residual + jnp.dot(mixed, w_out, preferred_element_type=jnp.float32)).astype(jnp.bfloat16)
    return lax.map(one_window, tokens)
```

```python
import functools

import jax
import jax.numpy as jnp
from jax import lax
from jax.experimental import pallas as pl
from jax.experimental.pallas import tpu as pltpu
from jax.sharding import PartitionSpec as P

HEADS = 8
HEAD_K = 128
HEAD_V = 192
KW_STEM = 15
KW = 5
POOL_A = 8
POOL_B = 16
GROUP = POOL_A * POOL_B
SPAN = 24

epsilon = 1e-06


def rms_scale(values, gain):
    return values * lax.rsqrt(jnp.mean(values * values, axis=-1, keepdims=True) + epsilon) * gain


def rotate(values, angles):
    half_dim = values.shape[-1] // 2
    first = values[..., :half_dim]
    second = values[..., half_dim:]
    cosine = jnp.cos(angles)
    sine = jnp.sin(angles)
    return jnp.concatenate(
        [first * cosine - second * sine, second * cosine + first * sine], axis=-1
    )


def stem_kernel(
    tok_ref, low_ref, high_ref, weight_ref, bias_ref, gain_ref, ext_ref, text_ref, hot_ref, shifted_ref, rows_ref
):
    count = tok_ref.shape[0]
    channels = weight_ref.shape[1]
    place = lax.axis_index("seq")
    last_place = lax.axis_size("seq") - 1
    main = tok_ref[...].astype(jnp.float32)
    row = lax.broadcasted_iota(jnp.int32, main.shape, 0)
    previous = jnp.where(row == 0, low_ref[...].astype(jnp.float32), pltpu.roll(main, 1, 0))
    following = jnp.where(
        row == count - 1, high_ref[...].astype(jnp.float32), pltpu.roll(main, count - 1, 0)
    )
    text_ref[0:SPAN, :] = previous.T[GROUP - SPAN :, :]
    text_ref[SPAN : SPAN + GROUP, :] = main.T
    text_ref[SPAN + GROUP :, :] = following.T[:SPAN, :]

    source = lax.broadcasted_iota(jnp.int32, (GROUP, weight_ref.shape[0]), 1)
    target = lax.broadcasted_iota(jnp.int32, (GROUP, weight_ref.shape[0]), 0)
    tap = source // 4
    base = source - 4 * tap
    for offset in range(POOL_A):
        pick = (target == base * SPAN + offset + tap + 1).astype(jnp.float32).astype(jnp.bfloat16)
        shifted_ref[offset] = jnp.dot(
            pick, weight_ref[...], preferred_element_type=jnp.float32
        ).astype(jnp.bfloat16)

    def hot_of(span):
        planes = [(span == float(code)).astype(jnp.float32) for code in range(1, 5)]
        planes.append(jnp.zeros((GROUP - 4 * SPAN, span.shape[1]), jnp.float32))
        return jnp.concatenate(planes, axis=0).T.astype(jnp.bfloat16)

    for j in range(POOL_B):
        hot_ref[j] = hot_of(text_ref[8 * j + SPAN - 8 : 8 * j + 2 * SPAN - 8, :])
    lane = lax.broadcasted_iota(jnp.int32, (SPAN, count), 1)
    edge = jnp.where(
        lane == 0,
        text_ref[0:SPAN, :],
        jnp.where(
            lane == 1,
            pltpu.roll(text_ref[8 : 8 + SPAN, :], 1, 1),
            jnp.where(
                lane == 2,
                pltpu.roll(text_ref[GROUP + SPAN - 8 : GROUP + 2 * SPAN - 8, :], 3, 1),
                pltpu.roll(text_ref[GROUP + SPAN : GROUP + 2 * SPAN, :], 4, 1),
            ),
        ),
    )
    hot_ref[POOL_B] = hot_of(edge)

    width = 256

    def block(j, carry):
        hot = hot_ref[j]
        for chunk in range(channels // width):
            columns = slice(chunk * width, (chunk + 1) * width)
            best = None
            for offset in range(POOL_A):
                stem = jnp.dot(
                    hot, shifted_ref[offset, :, columns], preferred_element_type=jnp.float32
                )
                best = stem if best is None else jnp.maximum(best, stem)
            pooled = jax.nn.gelu(best + bias_ref[:, columns]).astype(jnp.bfloat16)
            rows_ref[:, columns] = pooled.astype(jnp.float32)
        pooled = rows_ref[...]
        start = pl.multiple_of((j + 2) * count, count)
        ext_ref[pl.ds(start, count), :] = rms_scale(pooled, gain_ref[...]).astype(jnp.bfloat16)
        return carry

    lax.fori_loop(0, POOL_B + 1, block, 0)
    edges = ext_ref[(POOL_B + 2) * count : (POOL_B + 3) * count, :].astype(jnp.float32)
    left_keep = (place > 0).astype(jnp.float32)
    right_keep = (place < last_place).astype(jnp.float32)
    spot = lax.broadcasted_iota(jnp.int32, (count, channels), 0)
    for index in range(2):
        inner = ext_ref[(POOL_B + index) * count : (POOL_B + index + 1) * count, :]
        moved = pltpu.roll(inner.astype(jnp.float32), 1, 0)
        ext_ref[index * count : (index + 1) * count, :] = jnp.where(
            spot == 0, edges[index : index + 1, :] * left_keep, moved
        ).astype(jnp.bfloat16)
        inner = ext_ref[(2 + index) * count : (3 + index) * count, :]
        moved = pltpu.roll(inner.astype(jnp.float32), count - 1, 0)
        at = POOL_B + 2 + index
        ext_ref[at * count : (at + 1) * count, :] = jnp.where(
            spot == count - 1, edges[2 + index : 3 + index, :] * right_keep, moved
        ).astype(jnp.bfloat16)


def stem_stage(tokens, low, high, stem_weight, stem_bias, conv_gain):
    count = tokens.shape[0]
    channels = stem_weight.shape[1]
    return pl.pallas_call(
        stem_kernel,
        out_shape=jax.ShapeDtypeStruct(((POOL_B + 4) * count, channels), jnp.bfloat16),
        in_specs=[pl.BlockSpec(memory_space=pltpu.VMEM)] * 6,
        out_specs=pl.BlockSpec(memory_space=pltpu.VMEM),
        scratch_shapes=[
            pltpu.VMEM((GROUP + 2 * SPAN, count), jnp.float32),
            pltpu.VMEM((POOL_B + 1, count, GROUP), jnp.bfloat16),
            pltpu.VMEM((POOL_A, GROUP, channels), jnp.bfloat16),
            pltpu.VMEM((count, channels), jnp.float32),
        ],
        cost_estimate=pl.CostEstimate(
            flops=20_000_000_000, bytes_accessed=4_000_000, transcendentals=1_600_000
        ),
        name="stem_stage",
    )(tokens, low, high, stem_weight, stem_bias[None], conv_gain[None])


def conv_kernel(count, ext_ref, weight_ref, bias_ref, coarse_ref):
    group = 4
    width = weight_ref.shape[-1]
    channels = ext_ref.shape[1]

    def block(m, carry):
        most, least = carry
        total = None
        for tap in range(KW):
            start = pl.multiple_of((m * group + tap) * count, count)
            part = jnp.dot(
                ext_ref[pl.ds(start, group * count), :],
                weight_ref[:, :, 0, tap].reshape(channels, width),
                preferred_element_type=jnp.float32,
            )
            total = part if total is None else total + part
        for index in range(group):
            piece = total[index * count : (index + 1) * count]
            most = jnp.maximum(most, piece)
            least = jnp.minimum(least, piece)
        return most, least

    big = jnp.full((count, width), jnp.finfo(jnp.float32).max, jnp.float32)
    most, least = lax.fori_loop(0, POOL_B // group, block, (-big, big))
    bias = bias_ref[...]
    coarse_ref[...] = jnp.maximum(jax.nn.gelu(most + bias), jax.nn.gelu(least + bias)).astype(
        jnp.bfloat16
    )


def conv_stage(ext, weight, conv_bias):
    count = ext.shape[0] // (POOL_B + 4)
    ways, row_parts, column_parts, taps, depth, columns = weight.shape
    width = 256
    steps = columns // width
    return pl.pallas_call(
        functools.partial(conv_kernel, count),
        grid=(column_parts, steps),
        out_shape=jax.ShapeDtypeStruct((count, column_parts * columns), jnp.bfloat16),
        in_specs=[
            pl.BlockSpec(ext.shape, lambda b, n: (0, 0), pipeline_mode=pl.Buffered(1)),
            pl.BlockSpec(
                (ways, row_parts, 1, taps, depth, width), lambda b, n: (0, 0, b, 0, 0, n)
            ),
            pl.BlockSpec((1, width), lambda b, n: (0, b * steps + n)),
        ],
        out_specs=pl.BlockSpec((count, width), lambda b, n: (0, b * steps + n)),
        cost_estimate=pl.CostEstimate(
            flops=24_000_000_000, bytes_accessed=16_000_000, transcendentals=400_000
        ),
        name="conv_stage",
    )(ext, weight, conv_bias[None])


def gather_conv(conv_weight):
    taps, depth, columns = conv_weight.shape
    members = lax.axis_size("seq")
    place = lax.axis_index("seq")
    for row_parts in (2, 1, 3):
        column_parts = members // row_parts
        if members % row_parts or depth % (16 * row_parts) or columns % (256 * column_parts):
            continue
        depth_part = depth // row_parts
        column_part = columns // column_parts
        piece = lax.dynamic_slice(
            conv_weight,
            (0, place // column_parts * depth_part, place % column_parts * column_part),
            (taps, depth_part, column_part),
        )
        full = lax.all_gather(piece, ("dp", "seq"), axis=0, tiled=False)
        return full.reshape(-1, row_parts, column_parts, taps, depth_part, column_part)
    full = lax.all_gather(conv_weight, "dp", axis=0, tiled=False)
    return full[:, None, None]


def gather_rows(weight):
    members = lax.axis_size("seq")
    rows = weight.shape[0] // members
    piece = lax.dynamic_slice_in_dim(weight, lax.axis_index("seq") * rows, rows, axis=0)
    return lax.all_gather(piece, ("dp", "seq"), axis=0, tiled=True)


def body(
    tokens,
    stem_weight,
    stem_bias,
    conv_gain,
    conv_weight,
    conv_bias,
    attn_gain,
    w_query,
    w_key,
    w_value,
    w_out,
):
    seq_local = tokens.shape[1]
    rows_att = seq_local // GROUP
    full_conv = gather_conv(conv_weight)
    projections = gather_rows(jnp.concatenate([w_query, w_key, w_value], axis=1))
    full_out = gather_rows(w_out)
    tokens = tokens.reshape(rows_att, GROUP)
    size = lax.axis_size("seq")
    forward = [(i, i + 1) for i in range(size - 1)]
    backward = [(i + 1, i) for i in range(size - 1)]
    low = lax.ppermute(tokens[-1:], "seq", forward)
    high = lax.ppermute(tokens[:1], "seq", backward)
    ext = stem_stage(tokens, low, high, stem_weight, stem_bias, conv_gain)
    coarse = conv_stage(ext, full_conv, conv_bias)
    residual = coarse.astype(jnp.float32)
    hidden = rms_scale(residual, attn_gain).astype(jnp.bfloat16)
    projected = jnp.dot(hidden, projections, preferred_element_type=jnp.float32)
    split = HEADS * HEAD_K
    query = projected[:, :split]
    keys = projected[:, split : split + HEAD_K]
    values = projected[:, split + HEAD_K :]
    half_dim = HEAD_K // 2
    freqs = 10000.0 ** (-jnp.arange(half_dim, dtype=jnp.float32) / half_dim)
    positions = lax.axis_index("seq") * rows_att + jnp.arange(rows_att, dtype=jnp.int32)
    angles = positions.astype(jnp.float32)[:, None] * freqs[None, :]
    query = rotate(query.reshape(rows_att, HEADS, HEAD_K), angles[:, None, :]).astype(jnp.bfloat16)
    keys = rotate(keys, angles).astype(jnp.bfloat16)
    pair = jnp.concatenate([keys, values.astype(jnp.bfloat16)], axis=1)
    pair = lax.all_gather(pair, "seq", axis=0, tiled=True)
    keys_all, values_all = pair[:, :HEAD_K], pair[:, HEAD_K:]
    scores = jnp.einsum(
        "rhd,kd->hrk", query, keys_all, preferred_element_type=jnp.float32
    ) * HEAD_K ** (-0.5)
    weights = jax.nn.softmax(scores, axis=-1).astype(jnp.bfloat16)
    mixed = jnp.einsum(
        "hrk,kd->rhd", weights, values_all, preferred_element_type=jnp.float32
    ).astype(jnp.bfloat16)
    mixed = mixed.reshape(rows_att, HEADS * HEAD_V)
    out = jnp.dot(mixed, full_out, preferred_element_type=jnp.float32)
    return (residual + out).astype(jnp.bfloat16)[None]


def solution(mesh):
    in_specs = (
        P("dp", "seq"),
        P(),
        P(),
        P(),
        P(None, "dp", None),
        P(),
        P(),
        P("dp", None),
        P("dp", None),
        P("dp", None),
        P("dp", None),
    )
    out_specs = P("dp", "seq", None)
    return jax.shard_map(body, mesh=mesh, in_specs=in_specs, out_specs=out_specs, check_vma=False)
```

```python
import functools

import jax
import jax.numpy as jnp
from jax import lax
from jax.experimental import pallas as pl
from jax.experimental.pallas import tpu as pltpu
from jax.sharding import PartitionSpec as P

HEADS = 8
HEAD_K = 128
HEAD_V = 192
KW_STEM = 15
KW = 5
POOL_A = 8
POOL_B = 16
GROUP = POOL_A * POOL_B
SPAN = 24

epsilon = 1e-06


def rms_scale(values, gain):
    return values * lax.rsqrt(jnp.mean(values * values, axis=-1, keepdims=True) + epsilon) * gain


def rotate(values, angles):
    half_dim = values.shape[-1] // 2
    first = values[..., :half_dim]
    second = values[..., half_dim:]
    cosine = jnp.cos(angles)
    sine = jnp.sin(angles)
    return jnp.concatenate(
        [first * cosine - second * sine, second * cosine + first * sine], axis=-1
    )


def stem_kernel(
    tok_ref, low_ref, high_ref, weight_ref, bias_ref, gain_ref, ext_ref, text_ref, hot_ref, shifted_ref, rows_ref
):
    stem_compute(
        tok_ref,
        low_ref[...],
        high_ref[...],
        weight_ref,
        bias_ref,
        gain_ref,
        ext_ref,
        text_ref,
        hot_ref,
        shifted_ref,
        rows_ref,
    )


def stem_compute(
    tok_ref, low, high, weight_ref, bias_ref, gain_ref, ext_ref, text_ref, hot_ref, shifted_ref, rows_ref
):
    count = tok_ref.shape[0]
    channels = weight_ref.shape[1]
    place = lax.axis_index("seq")
    last_place = lax.axis_size("seq") - 1
    main = tok_ref[...].astype(jnp.float32)
    row = lax.broadcasted_iota(jnp.int32, main.shape, 0)
    previous = jnp.where(row == 0, low.astype(jnp.float32), pltpu.roll(main, 1, 0))
    following = jnp.where(
        row == count - 1, high.astype(jnp.float32), pltpu.roll(main, count - 1, 0)
    )
    text_ref[0:SPAN, :] = previous.T[GROUP - SPAN :, :]
    text_ref[SPAN : SPAN + GROUP, :] = main.T
    text_ref[SPAN + GROUP :, :] = following.T[:SPAN, :]

    source = lax.broadcasted_iota(jnp.int32, (GROUP, weight_ref.shape[0]), 1)
    target = lax.broadcasted_iota(jnp.int32, (GROUP, weight_ref.shape[0]), 0)
    tap = source // 4
    base = source - 4 * tap
    for offset in range(POOL_A):
        pick = (target == base * SPAN + offset + tap + 1).astype(jnp.float32).astype(jnp.bfloat16)
        shifted_ref[offset] = jnp.dot(
            pick, weight_ref[...], preferred_element_type=jnp.float32
        ).astype(jnp.bfloat16)

    def hot_of(span):
        planes = [(span == float(code)).astype(jnp.float32) for code in range(1, 5)]
        planes.append(jnp.zeros((GROUP - 4 * SPAN, span.shape[1]), jnp.float32))
        return jnp.concatenate(planes, axis=0).T.astype(jnp.bfloat16)

    for j in range(POOL_B):
        hot_ref[j] = hot_of(text_ref[8 * j + SPAN - 8 : 8 * j + 2 * SPAN - 8, :])
    lane = lax.broadcasted_iota(jnp.int32, (SPAN, count), 1)
    edge = jnp.where(
        lane == 0,
        text_ref[0:SPAN, :],
        jnp.where(
            lane == 1,
            pltpu.roll(text_ref[8 : 8 + SPAN, :], 1, 1),
            jnp.where(
                lane == 2,
                pltpu.roll(text_ref[GROUP + SPAN - 8 : GROUP + 2 * SPAN - 8, :], 3, 1),
                pltpu.roll(text_ref[GROUP + SPAN : GROUP + 2 * SPAN, :], 4, 1),
            ),
        ),
    )
    hot_ref[POOL_B] = hot_of(edge)

    width = 256

    def block(j, carry):
        hot = hot_ref[j]
        for chunk in range(channels // width):
            columns = slice(chunk * width, (chunk + 1) * width)
            best = None
            for offset in range(POOL_A):
                stem = jnp.dot(
                    hot, shifted_ref[offset, :, columns], preferred_element_type=jnp.float32
                )
                best = stem if best is None else jnp.maximum(best, stem)
            pooled = jax.nn.gelu(best + bias_ref[:, columns]).astype(jnp.bfloat16)
            rows_ref[:, columns] = pooled.astype(jnp.float32)
        pooled = rows_ref[...]
        start = pl.multiple_of((j + 2) * count, count)
        ext_ref[pl.ds(start, count), :] = rms_scale(pooled, gain_ref[...]).astype(jnp.bfloat16)
        return carry

    lax.fori_loop(0, POOL_B + 1, block, 0)
    edges = ext_ref[(POOL_B + 2) * count : (POOL_B + 3) * count, :].astype(jnp.float32)
    left_keep = (place > 0).astype(jnp.float32)
    right_keep = (place < last_place).astype(jnp.float32)
    spot = lax.broadcasted_iota(jnp.int32, (count, channels), 0)
    for index in range(2):
        inner = ext_ref[(POOL_B + index) * count : (POOL_B + index + 1) * count, :]
        moved = pltpu.roll(inner.astype(jnp.float32), 1, 0)
        ext_ref[index * count : (index + 1) * count, :] = jnp.where(
            spot == 0, edges[index : index + 1, :] * left_keep, moved
        ).astype(jnp.bfloat16)
        inner = ext_ref[(2 + index) * count : (3 + index) * count, :]
        moved = pltpu.roll(inner.astype(jnp.float32), count - 1, 0)
        at = POOL_B + 2 + index
        ext_ref[at * count : (at + 1) * count, :] = jnp.where(
            spot == count - 1, edges[2 + index : 3 + index, :] * right_keep, moved
        ).astype(jnp.bfloat16)


def stem_stage(tokens, low, high, stem_weight, stem_bias, conv_gain):
    count = tokens.shape[0]
    channels = stem_weight.shape[1]
    return pl.pallas_call(
        stem_kernel,
        out_shape=jax.ShapeDtypeStruct(((POOL_B + 4) * count, channels), jnp.bfloat16),
        in_specs=[pl.BlockSpec(memory_space=pltpu.VMEM)] * 6,
        out_specs=pl.BlockSpec(memory_space=pltpu.VMEM),
        scratch_shapes=[
            pltpu.VMEM((GROUP + 2 * SPAN, count), jnp.float32),
            pltpu.VMEM((POOL_B + 1, count, GROUP), jnp.bfloat16),
            pltpu.VMEM((POOL_A, GROUP, channels), jnp.bfloat16),
            pltpu.VMEM((count, channels), jnp.float32),
        ],
        cost_estimate=pl.CostEstimate(
            flops=20_000_000_000, bytes_accessed=4_000_000, transcendentals=1_600_000
        ),
        name="stem_stage",
    )(tokens, low, high, stem_weight, stem_bias[None], conv_gain[None])


def conv_kernel(count, ext_ref, weight_ref, bias_ref, coarse_ref):
    group = 4
    width = weight_ref.shape[-1]
    channels = ext_ref.shape[1]

    def block(m, carry):
        most, least = carry
        total = None
        for tap in range(KW):
            start = pl.multiple_of((m * group + tap) * count, count)
            part = jnp.dot(
                ext_ref[pl.ds(start, group * count), :],
                weight_ref[:, :, 0, tap].reshape(channels, width),
                preferred_element_type=jnp.float32,
            )
            total = part if total is None else total + part
        for index in range(group):
            piece = total[index * count : (index + 1) * count]
            most = jnp.maximum(most, piece)
            least = jnp.minimum(least, piece)
        return most, least

    big = jnp.full((count, width), jnp.finfo(jnp.float32).max, jnp.float32)
    most, least = lax.fori_loop(0, POOL_B // group, block, (-big, big))
    bias = bias_ref[...]
    coarse_ref[...] = jnp.maximum(jax.nn.gelu(most + bias), jax.nn.gelu(least + bias)).astype(
        jnp.bfloat16
    )


def conv_stage(ext, weight, conv_bias):
    count = ext.shape[0] // (POOL_B + 4)
    ways, row_parts, column_parts, taps, depth, columns = weight.shape
    width = 256
    steps = columns // width
    return pl.pallas_call(
        functools.partial(conv_kernel, count),
        grid=(column_parts, steps),
        out_shape=jax.ShapeDtypeStruct((count, column_parts * columns), jnp.bfloat16),
        in_specs=[
            pl.BlockSpec(ext.shape, lambda b, n: (0, 0), pipeline_mode=pl.Buffered(1)),
            pl.BlockSpec(
                (ways, row_parts, 1, taps, depth, width), lambda b, n: (0, 0, b, 0, 0, n)
            ),
            pl.BlockSpec((1, width), lambda b, n: (0, b * steps + n)),
        ],
        out_specs=pl.BlockSpec((count, width), lambda b, n: (0, b * steps + n)),
        cost_estimate=pl.CostEstimate(
            flops=24_000_000_000, bytes_accessed=16_000_000, transcendentals=400_000
        ),
        name="conv_stage",
    )(ext, weight, conv_bias[None])


MESH = pl.DeviceIdType.MESH


def encoder_kernel(
    tok_ref,
    stem_weight_ref,
    stem_bias_ref,
    gain_ref,
    conv_bias_ref,
    conv_ref,
    attn_ref,
    coarse_ref,
    full_attn_ref,
    text_ref,
    hot_ref,
    shifted_ref,
    rows_ref,
    ext_ref,
    low_ref,
    high_ref,
    conv_full,
    attn_full,
    halo_send,
    halo_recv,
    send_sem,
    recv_sem,
    local_sem,
    out_sem,
):
    ways = lax.axis_size("dp")
    members = lax.axis_size("seq")
    chips = ways // 2
    me = lax.axis_index("dp")
    place = lax.axis_index("seq")
    chip = me // 2
    core = me % 2
    partner = chip * 2 + 1 - core
    count = tok_ref.shape[0]
    _, row_parts, column_parts, _, _, columns = conv_full.shape
    depth = conv_full.shape[4]

    def peer_of(step):
        return (chip + step) % chips * 2 + core

    barrier = pltpu.get_barrier_semaphore()
    pl.semaphore_signal(barrier, inc=1, device_id=(partner, place), device_id_type=MESH)
    for step in range(1, chips):
        pl.semaphore_signal(
            barrier, inc=1, device_id=(peer_of(step), place), device_id_type=MESH
        )
    for turn in range(1, members):
        pl.semaphore_signal(
            barrier, inc=1, device_id=(me, (place + turn) % members), device_id_type=MESH
        )
    pl.semaphore_wait(barrier, 1 + (chips - 1) + (members - 1))

    right = (place + 1) % members
    left = (place + members - 1) % members
    halo = [
        pltpu.make_async_remote_copy(
            tok_ref.at[count - 8 : count], low_ref, halo_send.at[0], halo_recv.at[0], (me, right), MESH
        ),
        pltpu.make_async_remote_copy(
            tok_ref.at[0:8], high_ref, halo_send.at[1], halo_recv.at[1], (me, left), MESH
        ),
    ]
    for copy in halo:
        copy.start()

    def conv_source(spot):
        rows = pl.multiple_of(spot // column_parts * depth, depth)
        at = pl.multiple_of(spot % column_parts * columns, columns)
        return conv_ref.at[:, pl.ds(rows, depth), pl.ds(at, columns)]

    def conv_slot(way, spot):
        return conv_full.at[way, spot // column_parts, spot % column_parts]

    def attn_source(spot):
        return attn_ref.at[spot]

    def attn_slot(way, spot):
        return attn_full.at[way, spot]

    kinds = ((conv_source, conv_slot), (attn_source, attn_slot))
    sent = ([], [])
    local = ([], [])

    def send(kind, source, way, spot, target):
        copy = pltpu.make_async_remote_copy(
            source,
            kinds[kind][1](way, spot),
            send_sem.at[kind, len(sent[kind])],
            recv_sem.at[kind, way, spot],
            target,
            MESH,
        )
        copy.start()
        sent[kind].append(copy)

    def arrived(kind, way, spot):
        slot = kinds[kind][1](way, spot)
        pltpu.make_async_remote_copy(
            slot, slot, send_sem.at[kind, 0], recv_sem.at[kind, way, spot], (partner, place), MESH
        ).wait_recv()

    def first(kind):
        source, slot = kinds[kind]
        for step in range(1, chips):
            send(kind, source(place), me, place, (peer_of(step), place))
        for spot in range(members):
            send(kind, source(spot), me, spot, (partner, place))
            copy = pltpu.make_async_copy(source(spot), slot(me, spot), local_sem.at[kind, spot])
            copy.start()
            local[kind].append(copy)

    order = sorted(range(1, chips), key=lambda step: min(step, chips - step))

    def second(kind):
        slot = kinds[kind][1]
        for step in order:
            way = peer_of(step)
            arrived(kind, way, place)
            for turn in range(1, members):
                send(kind, slot(way, place), way, place, (me, (place + turn) % members))
            send(kind, slot(way, place), way, place, (partner, place))

    def third(kind):
        slot = kinds[kind][1]
        for step in order:
            way = peer_of(step)
            for turn in range(1, members):
                spot = (place + turn) % members
                arrived(kind, way, spot)
                send(kind, slot(way, spot), way, spot, (partner, place))

    def finish(kind):
        for step in range(chips):
            way = (chip + step) % chips * 2 + 1 - core
            for spot in range(members):
                arrived(kind, way, spot)
        for copy in local[kind]:
            copy.wait()
        for copy in sent[kind]:
            copy.wait_send()

    first(0)
    for copy in halo:
        copy.wait()
    low = jnp.where(place > 0, low_ref[7:8], 0)
    high = jnp.where(place < members - 1, high_ref[0:1], 0)
    stem_compute(
        tok_ref,
        low,
        high,
        stem_weight_ref,
        stem_bias_ref,
        gain_ref,
        ext_ref,
        text_ref,
        hot_ref,
        shifted_ref,
        rows_ref,
    )
    second(0)
    first(1)
    third(0)
    finish(0)

    width = 256
    steps = columns // width
    group = 4
    channels = ext_ref.shape[1]
    big = jnp.full((count, width), jnp.finfo(jnp.float32).max, jnp.float32)

    def panel(index, nothing):
        b = index // steps
        inner = pl.multiple_of(index % steps * width, width)

        def block(m, carry):
            most, least = carry
            total = None
            for tap in range(KW):
                start = pl.multiple_of((m * group + tap) * count, count)
                part = jnp.dot(
                    ext_ref[pl.ds(start, group * count), :],
                    conv_full[:, :, b, tap, :, pl.ds(inner, width)].reshape(channels, width),
                    preferred_element_type=jnp.float32,
                )
                total = part if total is None else total + part
            for piece_index in range(group):
                piece = total[piece_index * count : (piece_index + 1) * count]
                most = jnp.maximum(most, piece)
                least = jnp.minimum(least, piece)
            return most, least

        most, least = lax.fori_loop(0, POOL_B // group, block, (-big, big))
        at = pl.multiple_of(index * width, width)
        bias = conv_bias_ref[:, pl.ds(at, width)]
        coarse_ref[:, pl.ds(at, width)] = jnp.maximum(
            jax.nn.gelu(most + bias), jax.nn.gelu(least + bias)
        ).astype(jnp.bfloat16)
        return nothing

    panels = column_parts * steps
    early = panels // 3
    lax.fori_loop(0, early, panel, 0)
    second(1)
    lax.fori_loop(early, panels, panel, 0)
    third(1)
    finish(1)
    out = pltpu.make_async_copy(attn_full, full_attn_ref, out_sem)
    out.start()
    out.wait()


def row_parts_of(depth, columns, members):
    for row_parts in (2, 1, 3):
        column_parts = members // row_parts
        if members % row_parts or depth % (16 * row_parts) or columns % (256 * column_parts):
            continue
        return row_parts, column_parts
    return None


def encoder_stage(tokens, stem_weight, stem_bias, conv_gain, conv_bias, conv_weight, attn_rows, parts):
    count = tokens.shape[0]
    channels = stem_weight.shape[1]
    taps, depth, columns = conv_weight.shape
    ways = lax.axis_size("dp")
    members = lax.axis_size("seq")
    row_parts, column_parts = parts
    copies = (ways // 2 - 1) * (2 * members) + members + ways
    full_attn = (ways,) + attn_rows.shape
    vmem = pl.BlockSpec(memory_space=pltpu.VMEM)
    hbm = pl.BlockSpec(memory_space=pl.ANY)
    return pl.pallas_call(
        encoder_kernel,
        out_shape=(
            jax.ShapeDtypeStruct((count, columns), jnp.bfloat16),
            jax.ShapeDtypeStruct(full_attn, jnp.bfloat16),
        ),
        in_specs=[vmem] * 5 + [hbm] * 2,
        out_specs=(vmem, hbm),
        scratch_shapes=[
            pltpu.VMEM((GROUP + 2 * SPAN, count), jnp.float32),
            pltpu.VMEM((POOL_B + 1, count, GROUP), jnp.bfloat16),
            pltpu.VMEM((POOL_A, GROUP, channels), jnp.bfloat16),
            pltpu.VMEM((count, channels), jnp.float32),
            pltpu.VMEM(((POOL_B + 4) * count, channels), jnp.bfloat16),
            pltpu.VMEM((8, GROUP), jnp.int32),
            pltpu.VMEM((8, GROUP), jnp.int32),
            pltpu.VMEM(
                (ways, row_parts, column_parts, taps, depth // row_parts, columns // column_parts),
                jnp.bfloat16,
            ),
            pltpu.VMEM(full_attn, jnp.bfloat16),
            pltpu.SemaphoreType.DMA((2,)),
            pltpu.SemaphoreType.DMA((2,)),
            pltpu.SemaphoreType.DMA((2, copies)),
            pltpu.SemaphoreType.DMA((2, ways, members)),
            pltpu.SemaphoreType.DMA((2, members)),
            pltpu.SemaphoreType.DMA(()),
        ],
        compiler_params=pltpu.CompilerParams(
            collective_id=0, has_side_effects=True, vmem_limit_bytes=56 * 2**20
        ),
        name="encoder_stage",
    )(tokens, stem_weight, stem_bias[None], conv_gain[None], conv_bias[None], conv_weight, attn_rows)


def gather_conv(conv_weight):
    taps, depth, columns = conv_weight.shape
    members = lax.axis_size("seq")
    place = lax.axis_index("seq")
    for row_parts in (2, 1, 3):
        column_parts = members // row_parts
        if members % row_parts or depth % (16 * row_parts) or columns % (256 * column_parts):
            continue
        depth_part = depth // row_parts
        column_part = columns // column_parts
        piece = lax.dynamic_slice(
            conv_weight,
            (0, place // column_parts * depth_part, place % column_parts * column_part),
            (taps, depth_part, column_part),
        )
        full = lax.all_gather(piece, ("dp", "seq"), axis=0, tiled=False)
        return full.reshape(-1, row_parts, column_parts, taps, depth_part, column_part)
    full = lax.all_gather(conv_weight, "dp", axis=0, tiled=False)
    return full[:, None, None]


def gather_rows(weight):
    members = lax.axis_size("seq")
    rows = weight.shape[0] // members
    piece = lax.dynamic_slice_in_dim(weight, lax.axis_index("seq") * rows, rows, axis=0)
    return lax.all_gather(piece, ("dp", "seq"), axis=0, tiled=True)


def body(
    tokens,
    stem_weight,
    stem_bias,
    conv_gain,
    conv_weight,
    conv_bias,
    attn_gain,
    w_query,
    w_key,
    w_value,
    w_out,
):
    seq_local = tokens.shape[1]
    rows_att = seq_local // GROUP
    tokens = tokens.reshape(rows_att, GROUP)
    size = lax.axis_size("seq")
    rows = w_out.shape[0]
    parts = row_parts_of(conv_weight.shape[1], conv_weight.shape[2], size)
    split = HEADS * HEAD_K
    if parts is not None and rows % (16 * size) == 0:
        packed = jnp.concatenate([w_query, w_key, w_out, w_value], axis=1)
        coarse, full = encoder_stage(
            tokens,
            stem_weight,
            stem_bias,
            conv_gain,
            conv_bias,
            conv_weight,
            packed.reshape(size, rows // size, -1),
            parts,
        )
        full = full.reshape(-1, full.shape[-1])
        middle = split + HEAD_K
        wide = w_out.shape[1]
        first_rows = full[:, :middle]
        value_rows = full[:, middle + wide :]
        full_out = full[:, middle : middle + wide]
    else:
        full_conv = gather_conv(conv_weight)
        projections = gather_rows(jnp.concatenate([w_query, w_key, w_value], axis=1))
        first_rows = projections[:, : split + HEAD_K]
        value_rows = projections[:, split + HEAD_K :]
        full_out = gather_rows(w_out)
        forward = [(i, i + 1) for i in range(size - 1)]
        backward = [(i + 1, i) for i in range(size - 1)]
        low = lax.ppermute(tokens[-1:], "seq", forward)
        high = lax.ppermute(tokens[:1], "seq", backward)
        ext = stem_stage(tokens, low, high, stem_weight, stem_bias, conv_gain)
        coarse = conv_stage(ext, full_conv, conv_bias)
    residual = coarse.astype(jnp.float32)
    hidden = rms_scale(residual, attn_gain).astype(jnp.bfloat16)
    projected = jnp.dot(hidden, first_rows, preferred_element_type=jnp.float32)
    query = projected[:, :split]
    keys = projected[:, split:]
    values = jnp.dot(hidden, value_rows, preferred_element_type=jnp.float32)
    half_dim = HEAD_K // 2
    freqs = 10000.0 ** (-jnp.arange(half_dim, dtype=jnp.float32) / half_dim)
    positions = lax.axis_index("seq") * rows_att + jnp.arange(rows_att, dtype=jnp.int32)
    angles = positions.astype(jnp.float32)[:, None] * freqs[None, :]
    query = rotate(query.reshape(rows_att, HEADS, HEAD_K), angles[:, None, :]).astype(jnp.bfloat16)
    keys = rotate(keys, angles).astype(jnp.bfloat16)
    pair = jnp.concatenate([keys, values.astype(jnp.bfloat16)], axis=1)
    pair = lax.all_gather(pair, "seq", axis=0, tiled=True)
    keys_all, values_all = pair[:, :HEAD_K], pair[:, HEAD_K:]
    scores = jnp.einsum(
        "rhd,kd->hrk", query, keys_all, preferred_element_type=jnp.float32
    ) * HEAD_K ** (-0.5)
    weights = jax.nn.softmax(scores, axis=-1).astype(jnp.bfloat16)
    mixed = jnp.einsum(
        "hrk,kd->rhd", weights, values_all, preferred_element_type=jnp.float32
    ).astype(jnp.bfloat16)
    mixed = mixed.reshape(rows_att, HEADS * HEAD_V)
    out = jnp.dot(mixed, full_out, preferred_element_type=jnp.float32)
    return (residual + out).astype(jnp.bfloat16)[None]


def solution(mesh):
    in_specs = (
        P("dp", "seq"),
        P(),
        P(),
        P(),
        P(None, "dp", None),
        P(),
        P(),
        P("dp", None),
        P("dp", None),
        P("dp", None),
        P("dp", None),
    )
    out_specs = P("dp", "seq", None)
    return jax.shard_map(body, mesh=mesh, in_specs=in_specs, out_specs=out_specs, check_vma=False)
```

```python
import functools

import jax
import jax.numpy as jnp
from jax import lax
from jax.experimental import pallas as pl
from jax.experimental.pallas import tpu as pltpu
from jax.sharding import PartitionSpec as P

HEADS = 8
HEAD_K = 128
HEAD_V = 192
KW_STEM = 15
KW = 5
POOL_A = 8
POOL_B = 16
GROUP = POOL_A * POOL_B
SPAN = 24

epsilon = 1e-06


def rms_scale(values, gain):
    return values * lax.rsqrt(jnp.mean(values * values, axis=-1, keepdims=True) + epsilon) * gain


def rotate(values, angles):
    half_dim = values.shape[-1] // 2
    first = values[..., :half_dim]
    second = values[..., half_dim:]
    cosine = jnp.cos(angles)
    sine = jnp.sin(angles)
    return jnp.concatenate(
        [first * cosine - second * sine, second * cosine + first * sine], axis=-1
    )


def stem_kernel(
    tok_ref, low_ref, high_ref, weight_ref, bias_ref, gain_ref, ext_ref, text_ref, hot_ref, shifted_ref, rows_ref
):
    stem_compute(
        tok_ref,
        low_ref[...],
        high_ref[...],
        weight_ref,
        bias_ref,
        gain_ref,
        ext_ref,
        text_ref,
        hot_ref,
        shifted_ref,
        rows_ref,
    )


def stem_compute(
    tok_ref, low, high, weight_ref, bias_ref, gain_ref, ext_ref, text_ref, hot_ref, shifted_ref, rows_ref, between=None
):
    count = tok_ref.shape[0]
    channels = weight_ref.shape[1]
    place = lax.axis_index("seq")
    last_place = lax.axis_size("seq") - 1
    main = tok_ref[...].astype(jnp.float32)
    row = lax.broadcasted_iota(jnp.int32, main.shape, 0)
    previous = jnp.where(row == 0, low.astype(jnp.float32), pltpu.roll(main, 1, 0))
    following = jnp.where(
        row == count - 1, high.astype(jnp.float32), pltpu.roll(main, count - 1, 0)
    )
    text_ref[0:SPAN, :] = previous.T[GROUP - SPAN :, :]
    text_ref[SPAN : SPAN + GROUP, :] = main.T
    text_ref[SPAN + GROUP :, :] = following.T[:SPAN, :]

    source = lax.broadcasted_iota(jnp.int32, (GROUP, weight_ref.shape[0]), 1)
    target = lax.broadcasted_iota(jnp.int32, (GROUP, weight_ref.shape[0]), 0)
    tap = source // 4
    base = source - 4 * tap
    for offset in range(POOL_A):
        pick = (target == base * SPAN + offset + tap + 1).astype(jnp.float32).astype(jnp.bfloat16)
        shifted_ref[offset] = jnp.dot(
            pick, weight_ref[...], preferred_element_type=jnp.float32
        ).astype(jnp.bfloat16)

    def hot_of(span):
        planes = [(span == float(code)).astype(jnp.float32) for code in range(1, 5)]
        planes.append(jnp.zeros((GROUP - 4 * SPAN, span.shape[1]), jnp.float32))
        return jnp.concatenate(planes, axis=0).T.astype(jnp.bfloat16)

    for j in range(POOL_B):
        hot_ref[j] = hot_of(text_ref[8 * j + SPAN - 8 : 8 * j + 2 * SPAN - 8, :])
    lane = lax.broadcasted_iota(jnp.int32, (SPAN, count), 1)
    edge = jnp.where(
        lane == 0,
        text_ref[0:SPAN, :],
        jnp.where(
            lane == 1,
            pltpu.roll(text_ref[8 : 8 + SPAN, :], 1, 1),
            jnp.where(
                lane == 2,
                pltpu.roll(text_ref[GROUP + SPAN - 8 : GROUP + 2 * SPAN - 8, :], 3, 1),
                pltpu.roll(text_ref[GROUP + SPAN : GROUP + 2 * SPAN, :], 4, 1),
            ),
        ),
    )
    hot_ref[POOL_B] = hot_of(edge)

    width = 256

    def block(j, carry):
        hot = hot_ref[j]
        for chunk in range(channels // width):
            columns = slice(chunk * width, (chunk + 1) * width)
            best = None
            for offset in range(POOL_A):
                stem = jnp.dot(
                    hot, shifted_ref[offset, :, columns], preferred_element_type=jnp.float32
                )
                best = stem if best is None else jnp.maximum(best, stem)
            pooled = jax.nn.gelu(best + bias_ref[:, columns]).astype(jnp.bfloat16)
            rows_ref[:, columns] = pooled.astype(jnp.float32)
        pooled = rows_ref[...]
        start = pl.multiple_of((j + 2) * count, count)
        ext_ref[pl.ds(start, count), :] = rms_scale(pooled, gain_ref[...]).astype(jnp.bfloat16)
        return carry

    if between is None:
        lax.fori_loop(0, POOL_B + 1, block, 0)
    else:
        lax.fori_loop(0, POOL_B // 2, block, 0)
        between()
        lax.fori_loop(POOL_B // 2, POOL_B + 1, block, 0)
    edges = ext_ref[(POOL_B + 2) * count : (POOL_B + 3) * count, :].astype(jnp.float32)
    left_keep = (place > 0).astype(jnp.float32)
    right_keep = (place < last_place).astype(jnp.float32)
    spot = lax.broadcasted_iota(jnp.int32, (count, channels), 0)
    for index in range(2):
        inner = ext_ref[(POOL_B + index) * count : (POOL_B + index + 1) * count, :]
        moved = pltpu.roll(inner.astype(jnp.float32), 1, 0)
        ext_ref[index * count : (index + 1) * count, :] = jnp.where(
            spot == 0, edges[index : index + 1, :] * left_keep, moved
        ).astype(jnp.bfloat16)
        inner = ext_ref[(2 + index) * count : (3 + index) * count, :]
        moved = pltpu.roll(inner.astype(jnp.float32), count - 1, 0)
        at = POOL_B + 2 + index
        ext_ref[at * count : (at + 1) * count, :] = jnp.where(
            spot == count - 1, edges[2 + index : 3 + index, :] * right_keep, moved
        ).astype(jnp.bfloat16)


def stem_stage(tokens, low, high, stem_weight, stem_bias, conv_gain):
    count = tokens.shape[0]
    channels = stem_weight.shape[1]
    return pl.pallas_call(
        stem_kernel,
        out_shape=jax.ShapeDtypeStruct(((POOL_B + 4) * count, channels), jnp.bfloat16),
        in_specs=[pl.BlockSpec(memory_space=pltpu.VMEM)] * 6,
        out_specs=pl.BlockSpec(memory_space=pltpu.VMEM),
        scratch_shapes=[
            pltpu.VMEM((GROUP + 2 * SPAN, count), jnp.float32),
            pltpu.VMEM((POOL_B + 1, count, GROUP), jnp.bfloat16),
            pltpu.VMEM((POOL_A, GROUP, channels), jnp.bfloat16),
            pltpu.VMEM((count, channels), jnp.float32),
        ],
        cost_estimate=pl.CostEstimate(
            flops=20_000_000_000, bytes_accessed=4_000_000, transcendentals=1_600_000
        ),
        name="stem_stage",
    )(tokens, low, high, stem_weight, stem_bias[None], conv_gain[None])


def conv_kernel(count, ext_ref, weight_ref, bias_ref, coarse_ref):
    group = 4
    width = weight_ref.shape[-1]
    channels = ext_ref.shape[1]

    def block(m, carry):
        most, least = carry
        total = None
        for tap in range(KW):
            start = pl.multiple_of((m * group + tap) * count, count)
            part = jnp.dot(
                ext_ref[pl.ds(start, group * count), :],
                weight_ref[:, :, 0, tap].reshape(channels, width),
                preferred_element_type=jnp.float32,
            )
            total = part if total is None else total + part
        for index in range(group):
            piece = total[index * count : (index + 1) * count]
            most = jnp.maximum(most, piece)
            least = jnp.minimum(least, piece)
        return most, least

    big = jnp.full((count, width), jnp.finfo(jnp.float32).max, jnp.float32)
    most, least = lax.fori_loop(0, POOL_B // group, block, (-big, big))
    bias = bias_ref[...]
    coarse_ref[...] = jnp.maximum(jax.nn.gelu(most + bias), jax.nn.gelu(least + bias)).astype(
        jnp.bfloat16
    )


def conv_stage(ext, weight, conv_bias):
    count = ext.shape[0] // (POOL_B + 4)
    ways, row_parts, column_parts, taps, depth, columns = weight.shape
    width = 256
    steps = columns // width
    return pl.pallas_call(
        functools.partial(conv_kernel, count),
        grid=(column_parts, steps),
        out_shape=jax.ShapeDtypeStruct((count, column_parts * columns), jnp.bfloat16),
        in_specs=[
            pl.BlockSpec(ext.shape, lambda b, n: (0, 0), pipeline_mode=pl.Buffered(1)),
            pl.BlockSpec(
                (ways, row_parts, 1, taps, depth, width), lambda b, n: (0, 0, b, 0, 0, n)
            ),
            pl.BlockSpec((1, width), lambda b, n: (0, b * steps + n)),
        ],
        out_specs=pl.BlockSpec((count, width), lambda b, n: (0, b * steps + n)),
        cost_estimate=pl.CostEstimate(
            flops=24_000_000_000, bytes_accessed=16_000_000, transcendentals=400_000
        ),
        name="conv_stage",
    )(ext, weight, conv_bias[None])


MESH = pl.DeviceIdType.MESH


def encoder_kernel(
    tok_ref,
    stem_weight_ref,
    stem_bias_ref,
    gain_ref,
    conv_bias_ref,
    conv_ref,
    attn_ref,
    coarse_ref,
    full_attn_ref,
    text_ref,
    hot_ref,
    shifted_ref,
    rows_ref,
    ext_ref,
    low_ref,
    high_ref,
    conv_full,
    attn_full,
    halo_send,
    halo_recv,
    send_sem,
    recv_sem,
    half_sem,
    local_sem,
    out_sem,
):
    ways = lax.axis_size("dp")
    members = lax.axis_size("seq")
    chips = ways // 2
    me = lax.axis_index("dp")
    place = lax.axis_index("seq")
    chip = me // 2
    core = me % 2
    partner = chip * 2 + 1 - core
    count = tok_ref.shape[0]
    _, row_parts, column_parts, _, _, columns = conv_full.shape
    depth = conv_full.shape[4]

    def peer_of(step):
        return (chip + step) % chips * 2 + core

    barrier = pltpu.get_barrier_semaphore()
    pl.semaphore_signal(barrier, inc=1, device_id=(partner, place), device_id_type=MESH)
    for step in range(1, chips):
        pl.semaphore_signal(
            barrier, inc=1, device_id=(peer_of(step), place), device_id_type=MESH
        )
    for turn in range(1, members):
        pl.semaphore_signal(
            barrier, inc=1, device_id=(me, (place + turn) % members), device_id_type=MESH
        )
    pl.semaphore_wait(barrier, 1 + (chips - 1) + (members - 1))

    right = (place + 1) % members
    left = (place + members - 1) % members
    halo = [
        pltpu.make_async_remote_copy(
            tok_ref.at[count - 8 : count], low_ref, halo_send.at[0], halo_recv.at[0], (me, right), MESH
        ),
        pltpu.make_async_remote_copy(
            tok_ref.at[0:8], high_ref, halo_send.at[1], halo_recv.at[1], (me, left), MESH
        ),
    ]
    for copy in halo:
        copy.start()

    def conv_source(spot):
        rows = pl.multiple_of(spot // column_parts * depth, depth)
        at = pl.multiple_of(spot % column_parts * columns, columns)
        return conv_ref.at[:, pl.ds(rows, depth), pl.ds(at, columns)]

    def conv_slot(way, spot):
        return conv_full.at[way, spot // column_parts, spot % column_parts]

    def attn_source(spot):
        return attn_ref.at[spot]

    def attn_slot(way, spot):
        return attn_full.at[way, spot]

    def conv_half(way, spot, half, turn):
        cut = columns // 256 * 128
        where = pl.ds(0, cut) if half == 0 else pl.ds(cut, columns - cut)
        return conv_full.at[way, spot // column_parts, spot % column_parts, :, :, where]

    def attn_half(way, spot, half, turn):
        rows = attn_ref.shape[1]
        tiles = rows // 16
        cut = (tiles // 2 if turn % 2 else tiles - tiles // 2) * 16
        where = pl.ds(0, cut) if half == 0 else pl.ds(cut, rows - cut)
        return attn_full.at[way, spot, where]

    kinds = ((conv_source, conv_slot, conv_half), (attn_source, attn_slot, attn_half))
    along_x = place + 1 - 2 * (place % 2)
    along_y = place + 2 - 4 * (place // 2)
    across = 3 - place
    sent = ([], [])
    local = ([], [])

    def send(kind, source, way, spot, target):
        copy = pltpu.make_async_remote_copy(
            source,
            kinds[kind][1](way, spot),
            send_sem.at[kind, len(sent[kind])],
            recv_sem.at[kind, way, spot],
            target,
            MESH,
        )
        copy.start()
        sent[kind].append(copy)

    def arrived(kind, way, spot):
        slot = kinds[kind][1](way, spot)
        pltpu.make_async_remote_copy(
            slot, slot, send_sem.at[kind, 0], recv_sem.at[kind, way, spot], (partner, place), MESH
        ).wait_recv()

    def first(kind):
        source, slot, _ = kinds[kind]
        for step in range(1, chips):
            send(kind, source(place), me, place, (peer_of(step), place))
        for spot in range(members):
            send(kind, source(spot), me, spot, (partner, place))
            copy = pltpu.make_async_copy(source(spot), slot(me, spot), local_sem.at[kind, spot])
            copy.start()
            local[kind].append(copy)

    order = sorted(range(1, chips), key=lambda step: min(step, chips - step))

    def second(kind, some):
        slot = kinds[kind][1]
        for step in some:
            way = peer_of(step)
            arrived(kind, way, place)
            send(kind, slot(way, place), way, place, (me, along_x))
            send(kind, slot(way, place), way, place, (me, along_y))
            send(kind, slot(way, place), way, place, (partner, place))

    def send_half(kind, way, spot, half, turn, target):
        ref = kinds[kind][2](way, spot, half, turn)
        copy = pltpu.make_async_remote_copy(
            ref,
            ref,
            send_sem.at[kind, len(sent[kind])],
            half_sem.at[kind, way, half],
            (me, target),
            MESH,
        )
        copy.start()
        sent[kind].append(copy)

    def third(kind):
        slot = kinds[kind][1]
        for turn, step in enumerate(order):
            way = peer_of(step)
            arrived(kind, way, along_x)
            send_half(kind, way, along_x, 0, turn, along_y)
            send(kind, slot(way, along_x), way, along_x, (partner, place))
            arrived(kind, way, along_y)
            send_half(kind, way, along_y, 1, turn, along_x)
            send(kind, slot(way, along_y), way, along_y, (partner, place))

    def fourth(kind):
        slot, half_of = kinds[kind][1:]
        for turn, step in enumerate(order):
            way = peer_of(step)
            for half in range(2):
                ref = half_of(way, across, half, turn)
                pltpu.make_async_remote_copy(
                    ref, ref, send_sem.at[kind, 0], half_sem.at[kind, way, half], (partner, place), MESH
                ).wait_recv()
            send(kind, slot(way, across), way, across, (partner, place))

    def finish(kind):
        for step in range(chips):
            way = (chip + step) % chips * 2 + 1 - core
            for spot in range(members):
                arrived(kind, way, spot)
        for copy in local[kind]:
            copy.wait()
        for copy in sent[kind]:
            copy.wait_send()

    first(0)
    for copy in halo:
        copy.wait()
    low = jnp.where(place > 0, low_ref[7:8], 0)
    high = jnp.where(place < members - 1, high_ref[0:1], 0)
    stem_compute(
        tok_ref,
        low,
        high,
        stem_weight_ref,
        stem_bias_ref,
        gain_ref,
        ext_ref,
        text_ref,
        hot_ref,
        shifted_ref,
        rows_ref,
        lambda: second(0, order[:1]),
    )
    second(0, order[1:])
    first(1)
    third(0)
    second(1, order[:1])
    fourth(0)
    second(1, order[1:])
    finish(0)

    width = 256
    steps = columns // width
    group = 4
    channels = ext_ref.shape[1]
    big = jnp.full((count, width), jnp.finfo(jnp.float32).max, jnp.float32)

    def panel(index, nothing):
        b = index // steps
        inner = pl.multiple_of(index % steps * width, width)

        def block(m, carry):
            most, least = carry
            total = None
            for tap in range(KW):
                start = pl.multiple_of((m * group + tap) * count, count)
                part = jnp.dot(
                    ext_ref[pl.ds(start, group * count), :],
                    conv_full[:, :, b, tap, :, pl.ds(inner, width)].reshape(channels, width),
                    preferred_element_type=jnp.float32,
                )
                total = part if total is None else total + part
            for piece_index in range(group):
                piece = total[piece_index * count : (piece_index + 1) * count]
                most = jnp.maximum(most, piece)
                least = jnp.minimum(least, piece)
            return most, least

        most, least = lax.fori_loop(0, POOL_B // group, block, (-big, big))
        at = pl.multiple_of(index * width, width)
        bias = conv_bias_ref[:, pl.ds(at, width)]
        coarse_ref[:, pl.ds(at, width)] = jnp.maximum(
            jax.nn.gelu(most + bias), jax.nn.gelu(least + bias)
        ).astype(jnp.bfloat16)
        return nothing

    panels = column_parts * steps
    early = panels // 2
    lax.fori_loop(0, early, panel, 0)
    third(1)
    lax.fori_loop(early, panels, panel, 0)
    fourth(1)
    finish(1)
    out = pltpu.make_async_copy(attn_full, full_attn_ref, out_sem)
    out.start()
    out.wait()


def row_parts_of(depth, columns, members):
    for row_parts in (2, 1, 3):
        column_parts = members // row_parts
        if members % row_parts or depth % (16 * row_parts) or columns % (256 * column_parts):
            continue
        return row_parts, column_parts
    return None


def encoder_stage(tokens, stem_weight, stem_bias, conv_gain, conv_bias, conv_weight, attn_rows, parts):
    count = tokens.shape[0]
    channels = stem_weight.shape[1]
    taps, depth, columns = conv_weight.shape
    ways = lax.axis_size("dp")
    members = lax.axis_size("seq")
    row_parts, column_parts = parts
    copies = (ways // 2 - 1) * (2 * members) + members + ways
    full_attn = (ways,) + attn_rows.shape
    vmem = pl.BlockSpec(memory_space=pltpu.VMEM)
    hbm = pl.BlockSpec(memory_space=pl.ANY)
    return pl.pallas_call(
        encoder_kernel,
        out_shape=(
            jax.ShapeDtypeStruct((count, columns), jnp.bfloat16),
            jax.ShapeDtypeStruct(full_attn, jnp.bfloat16),
        ),
        in_specs=[vmem] * 5 + [hbm] * 2,
        out_specs=(vmem, hbm),
        scratch_shapes=[
            pltpu.VMEM((GROUP + 2 * SPAN, count), jnp.float32),
            pltpu.VMEM((POOL_B + 1, count, GROUP), jnp.bfloat16),
            pltpu.VMEM((POOL_A, GROUP, channels), jnp.bfloat16),
            pltpu.VMEM((count, channels), jnp.float32),
            pltpu.VMEM(((POOL_B + 4) * count, channels), jnp.bfloat16),
            pltpu.VMEM((8, GROUP), jnp.int32),
            pltpu.VMEM((8, GROUP), jnp.int32),
            pltpu.VMEM(
                (ways, row_parts, column_parts, taps, depth // row_parts, columns // column_parts),
                jnp.bfloat16,
            ),
            pltpu.VMEM(full_attn, jnp.bfloat16),
            pltpu.SemaphoreType.DMA((2,)),
            pltpu.SemaphoreType.DMA((2,)),
            pltpu.SemaphoreType.DMA((2, copies)),
            pltpu.SemaphoreType.DMA((2, ways, members)),
            pltpu.SemaphoreType.DMA((2, ways, 2)),
            pltpu.SemaphoreType.DMA((2, members)),
            pltpu.SemaphoreType.DMA(()),
        ],
        compiler_params=pltpu.CompilerParams(
            collective_id=0, has_side_effects=True, vmem_limit_bytes=56 * 2**20
        ),
        name="encoder_stage",
    )(tokens, stem_weight, stem_bias[None], conv_gain[None], conv_bias[None], conv_weight, attn_rows)


def gather_conv(conv_weight):
    taps, depth, columns = conv_weight.shape
    members = lax.axis_size("seq")
    place = lax.axis_index("seq")
    for row_parts in (2, 1, 3):
        column_parts = members // row_parts
        if members % row_parts or depth % (16 * row_parts) or columns % (256 * column_parts):
            continue
        depth_part = depth // row_parts
        column_part = columns // column_parts
        piece = lax.dynamic_slice(
            conv_weight,
            (0, place // column_parts * depth_part, place % column_parts * column_part),
            (taps, depth_part, column_part),
        )
        full = lax.all_gather(piece, ("dp", "seq"), axis=0, tiled=False)
        return full.reshape(-1, row_parts, column_parts, taps, depth_part, column_part)
    full = lax.all_gather(conv_weight, "dp", axis=0, tiled=False)
    return full[:, None, None]


def gather_rows(weight):
    members = lax.axis_size("seq")
    rows = weight.shape[0] // members
    piece = lax.dynamic_slice_in_dim(weight, lax.axis_index("seq") * rows, rows, axis=0)
    return lax.all_gather(piece, ("dp", "seq"), axis=0, tiled=True)


def body(
    tokens,
    stem_weight,
    stem_bias,
    conv_gain,
    conv_weight,
    conv_bias,
    attn_gain,
    w_query,
    w_key,
    w_value,
    w_out,
):
    seq_local = tokens.shape[1]
    rows_att = seq_local // GROUP
    tokens = tokens.reshape(rows_att, GROUP)
    size = lax.axis_size("seq")
    rows = w_out.shape[0]
    parts = row_parts_of(conv_weight.shape[1], conv_weight.shape[2], size)
    split = HEADS * HEAD_K
    if size == 4 and parts is not None and rows % (16 * size) == 0:
        packed = jnp.concatenate([w_query, w_key, w_out, w_value], axis=1)
        coarse, full = encoder_stage(
            tokens,
            stem_weight,
            stem_bias,
            conv_gain,
            conv_bias,
            conv_weight,
            packed.reshape(size, rows // size, -1),
            parts,
        )
        full = full.reshape(-1, full.shape[-1])
        middle = split + HEAD_K
        wide = w_out.shape[1]
        first_rows = full[:, :middle]
        value_rows = full[:, middle + wide :]
        full_out = full[:, middle : middle + wide]
    else:
        full_conv = gather_conv(conv_weight)
        projections = gather_rows(jnp.concatenate([w_query, w_key, w_value], axis=1))
        first_rows = projections[:, : split + HEAD_K]
        value_rows = projections[:, split + HEAD_K :]
        full_out = gather_rows(w_out)
        forward = [(i, i + 1) for i in range(size - 1)]
        backward = [(i + 1, i) for i in range(size - 1)]
        low = lax.ppermute(tokens[-1:], "seq", forward)
        high = lax.ppermute(tokens[:1], "seq", backward)
        ext = stem_stage(tokens, low, high, stem_weight, stem_bias, conv_gain)
        coarse = conv_stage(ext, full_conv, conv_bias)
    residual = coarse.astype(jnp.float32)
    hidden = rms_scale(residual, attn_gain).astype(jnp.bfloat16)
    projected = jnp.dot(hidden, first_rows, preferred_element_type=jnp.float32)
    query = projected[:, :split]
    keys = projected[:, split:]
    values = jnp.dot(hidden, value_rows, preferred_element_type=jnp.float32)
    half_dim = HEAD_K // 2
    freqs = 10000.0 ** (-jnp.arange(half_dim, dtype=jnp.float32) / half_dim)
    positions = lax.axis_index("seq") * rows_att + jnp.arange(rows_att, dtype=jnp.int32)
    angles = positions.astype(jnp.float32)[:, None] * freqs[None, :]
    query = rotate(query.reshape(rows_att, HEADS, HEAD_K), angles[:, None, :]).astype(jnp.bfloat16)
    keys = rotate(keys, angles).astype(jnp.bfloat16)
    pair = jnp.concatenate([keys, values.astype(jnp.bfloat16)], axis=1)
    pair = lax.all_gather(pair, "seq", axis=0, tiled=True)
    keys_all, values_all = pair[:, :HEAD_K], pair[:, HEAD_K:]
    scores = jnp.einsum(
        "rhd,kd->hrk", query, keys_all, preferred_element_type=jnp.float32
    ) * HEAD_K ** (-0.5)
    weights = jax.nn.softmax(scores, axis=-1).astype(jnp.bfloat16)
    mixed = jnp.einsum(
        "hrk,kd->rhd", weights, values_all, preferred_element_type=jnp.float32
    ).astype(jnp.bfloat16)
    mixed = mixed.reshape(rows_att, HEADS * HEAD_V)
    out = jnp.dot(mixed, full_out, preferred_element_type=jnp.float32)
    return (residual + out).astype(jnp.bfloat16)[None]


def solution(mesh):
    in_specs = (
        P("dp", "seq"),
        P(),
        P(),
        P(),
        P(None, "dp", None),
        P(),
        P(),
        P("dp", None),
        P("dp", None),
        P("dp", None),
        P("dp", None),
    )
    out_specs = P("dp", "seq", None)
    return jax.shard_map(body, mesh=mesh, in_specs=in_specs, out_specs=out_specs, check_vma=False)
```

```python
import functools

import jax
import jax.numpy as jnp
from jax import lax
from jax.experimental import pallas as pl
from jax.experimental.pallas import tpu as pltpu
from jax.sharding import PartitionSpec as P

HEADS = 8
HEAD_K = 128
HEAD_V = 192
KW_STEM = 15
KW = 5
POOL_A = 8
POOL_B = 16
GROUP = POOL_A * POOL_B
SPAN = 24

epsilon = 1e-06


def rms_scale(values, gain):
    return values * lax.rsqrt(jnp.mean(values * values, axis=-1, keepdims=True) + epsilon) * gain


def rotate(values, angles):
    half_dim = values.shape[-1] // 2
    first = values[..., :half_dim]
    second = values[..., half_dim:]
    cosine = jnp.cos(angles)
    sine = jnp.sin(angles)
    return jnp.concatenate(
        [first * cosine - second * sine, second * cosine + first * sine], axis=-1
    )


def stem_kernel(
    tok_ref, low_ref, high_ref, weight_ref, bias_ref, gain_ref, ext_ref, text_ref, hot_ref, shifted_ref, rows_ref
):
    stem_compute(
        tok_ref,
        low_ref[...],
        high_ref[...],
        weight_ref,
        bias_ref,
        gain_ref,
        ext_ref,
        text_ref,
        hot_ref,
        shifted_ref,
        rows_ref,
    )


def stem_compute(
    tok_ref, low, high, weight_ref, bias_ref, gain_ref, ext_ref, text_ref, hot_ref, shifted_ref, rows_ref, between=None
):
    count = tok_ref.shape[0]
    channels = weight_ref.shape[1]
    place = lax.axis_index("seq")
    last_place = lax.axis_size("seq") - 1
    main = tok_ref[...].astype(jnp.float32)
    row = lax.broadcasted_iota(jnp.int32, main.shape, 0)
    previous = jnp.where(row == 0, low.astype(jnp.float32), pltpu.roll(main, 1, 0))
    following = jnp.where(
        row == count - 1, high.astype(jnp.float32), pltpu.roll(main, count - 1, 0)
    )
    text_ref[0:SPAN, :] = previous.T[GROUP - SPAN :, :]
    text_ref[SPAN : SPAN + GROUP, :] = main.T
    text_ref[SPAN + GROUP :, :] = following.T[:SPAN, :]

    source = lax.broadcasted_iota(jnp.int32, (GROUP, weight_ref.shape[0]), 1)
    target = lax.broadcasted_iota(jnp.int32, (GROUP, weight_ref.shape[0]), 0)
    tap = source // 4
    base = source - 4 * tap
    for offset in range(POOL_A):
        pick = (target == base * SPAN + offset + tap + 1).astype(jnp.float32).astype(jnp.bfloat16)
        shifted_ref[offset] = jnp.dot(
            pick, weight_ref[...], preferred_element_type=jnp.float32
        ).astype(jnp.bfloat16)

    def hot_of(span):
        planes = [(span == float(code)).astype(jnp.float32) for code in range(1, 5)]
        planes.append(jnp.zeros((GROUP - 4 * SPAN, span.shape[1]), jnp.float32))
        return jnp.concatenate(planes, axis=0).T.astype(jnp.bfloat16)

    for j in range(POOL_B):
        hot_ref[j] = hot_of(text_ref[8 * j + SPAN - 8 : 8 * j + 2 * SPAN - 8, :])
    lane = lax.broadcasted_iota(jnp.int32, (SPAN, count), 1)
    edge = jnp.where(
        lane == 0,
        text_ref[0:SPAN, :],
        jnp.where(
            lane == 1,
            pltpu.roll(text_ref[8 : 8 + SPAN, :], 1, 1),
            jnp.where(
                lane == 2,
                pltpu.roll(text_ref[GROUP + SPAN - 8 : GROUP + 2 * SPAN - 8, :], 3, 1),
                pltpu.roll(text_ref[GROUP + SPAN : GROUP + 2 * SPAN, :], 4, 1),
            ),
        ),
    )
    hot_ref[POOL_B] = hot_of(edge)

    width = 256

    def block(j, carry):
        hot = hot_ref[j]
        for chunk in range(channels // width):
            columns = slice(chunk * width, (chunk + 1) * width)
            best = None
            for offset in range(POOL_A):
                stem = jnp.dot(
                    hot, shifted_ref[offset, :, columns], preferred_element_type=jnp.float32
                )
                best = stem if best is None else jnp.maximum(best, stem)
            pooled = jax.nn.gelu(best + bias_ref[:, columns]).astype(jnp.bfloat16)
            rows_ref[:, columns] = pooled.astype(jnp.float32)
        pooled = rows_ref[...]
        start = pl.multiple_of((j + 2) * count, count)
        ext_ref[pl.ds(start, count), :] = rms_scale(pooled, gain_ref[...]).astype(jnp.bfloat16)
        return carry

    if between is None:
        lax.fori_loop(0, POOL_B + 1, block, 0)
    else:
        lax.fori_loop(0, POOL_B // 2, block, 0)
        between()
        lax.fori_loop(POOL_B // 2, POOL_B + 1, block, 0)
    edges = ext_ref[(POOL_B + 2) * count : (POOL_B + 3) * count, :].astype(jnp.float32)
    left_keep = (place > 0).astype(jnp.float32)
    right_keep = (place < last_place).astype(jnp.float32)
    spot = lax.broadcasted_iota(jnp.int32, (count, channels), 0)
    for index in range(2):
        inner = ext_ref[(POOL_B + index) * count : (POOL_B + index + 1) * count, :]
        moved = pltpu.roll(inner.astype(jnp.float32), 1, 0)
        ext_ref[index * count : (index + 1) * count, :] = jnp.where(
            spot == 0, edges[index : index + 1, :] * left_keep, moved
        ).astype(jnp.bfloat16)
        inner = ext_ref[(2 + index) * count : (3 + index) * count, :]
        moved = pltpu.roll(inner.astype(jnp.float32), count - 1, 0)
        at = POOL_B + 2 + index
        ext_ref[at * count : (at + 1) * count, :] = jnp.where(
            spot == count - 1, edges[2 + index : 3 + index, :] * right_keep, moved
        ).astype(jnp.bfloat16)


def stem_stage(tokens, low, high, stem_weight, stem_bias, conv_gain):
    count = tokens.shape[0]
    channels = stem_weight.shape[1]
    return pl.pallas_call(
        stem_kernel,
        out_shape=jax.ShapeDtypeStruct(((POOL_B + 4) * count, channels), jnp.bfloat16),
        in_specs=[pl.BlockSpec(memory_space=pltpu.VMEM)] * 6,
        out_specs=pl.BlockSpec(memory_space=pltpu.VMEM),
        scratch_shapes=[
            pltpu.VMEM((GROUP + 2 * SPAN, count), jnp.float32),
            pltpu.VMEM((POOL_B + 1, count, GROUP), jnp.bfloat16),
            pltpu.VMEM((POOL_A, GROUP, channels), jnp.bfloat16),
            pltpu.VMEM((count, channels), jnp.float32),
        ],
        cost_estimate=pl.CostEstimate(
            flops=20_000_000_000, bytes_accessed=4_000_000, transcendentals=1_600_000
        ),
        name="stem_stage",
    )(tokens, low, high, stem_weight, stem_bias[None], conv_gain[None])


def conv_kernel(count, ext_ref, weight_ref, bias_ref, coarse_ref):
    group = 4
    width = weight_ref.shape[-1]
    channels = ext_ref.shape[1]

    def block(m, carry):
        most, least = carry
        total = None
        for tap in range(KW):
            start = pl.multiple_of((m * group + tap) * count, count)
            part = jnp.dot(
                ext_ref[pl.ds(start, group * count), :],
                weight_ref[:, :, 0, tap].reshape(channels, width),
                preferred_element_type=jnp.float32,
            )
            total = part if total is None else total + part
        for index in range(group):
            piece = total[index * count : (index + 1) * count]
            most = jnp.maximum(most, piece)
            least = jnp.minimum(least, piece)
        return most, least

    big = jnp.full((count, width), jnp.finfo(jnp.float32).max, jnp.float32)
    most, least = lax.fori_loop(0, POOL_B // group, block, (-big, big))
    bias = bias_ref[...]
    coarse_ref[...] = jnp.maximum(jax.nn.gelu(most + bias), jax.nn.gelu(least + bias)).astype(
        jnp.bfloat16
    )


def conv_stage(ext, weight, conv_bias):
    count = ext.shape[0] // (POOL_B + 4)
    ways, row_parts, column_parts, taps, depth, columns = weight.shape
    width = 256
    steps = columns // width
    return pl.pallas_call(
        functools.partial(conv_kernel, count),
        grid=(column_parts, steps),
        out_shape=jax.ShapeDtypeStruct((count, column_parts * columns), jnp.bfloat16),
        in_specs=[
            pl.BlockSpec(ext.shape, lambda b, n: (0, 0), pipeline_mode=pl.Buffered(1)),
            pl.BlockSpec(
                (ways, row_parts, 1, taps, depth, width), lambda b, n: (0, 0, b, 0, 0, n)
            ),
            pl.BlockSpec((1, width), lambda b, n: (0, b * steps + n)),
        ],
        out_specs=pl.BlockSpec((count, width), lambda b, n: (0, b * steps + n)),
        cost_estimate=pl.CostEstimate(
            flops=24_000_000_000, bytes_accessed=16_000_000, transcendentals=400_000
        ),
        name="conv_stage",
    )(ext, weight, conv_bias[None])


MESH = pl.DeviceIdType.MESH


def encoder_kernel(
    tok_ref,
    stem_weight_ref,
    vector_ref,
    cosine_ref,
    sine_ref,
    conv_ref,
    attn_ref,
    out_ref,
    coarse_ref,
    key_ref,
    value_ref,
    pair_send,
    pair_recv,
    text_ref,
    hot_ref,
    shifted_ref,
    rows_ref,
    ext_ref,
    low_ref,
    high_ref,
    conv_full,
    attn_full,
    halo_send,
    halo_recv,
    send_sem,
    recv_sem,
    half_sem,
    local_sem,
):
    stem_wide = stem_weight_ref.shape[1]
    wide = out_ref.shape[1]
    stem_bias_ref = vector_ref.at[:, 0:stem_wide]
    gain_ref = vector_ref.at[:, stem_wide : 2 * stem_wide]
    conv_bias_ref = vector_ref.at[:, 2 * stem_wide : 2 * stem_wide + wide]
    attn_gain_ref = vector_ref.at[:, 2 * stem_wide + wide :]
    ways = lax.axis_size("dp")
    members = lax.axis_size("seq")
    chips = ways // 2
    me = lax.axis_index("dp")
    place = lax.axis_index("seq")
    chip = me // 2
    core = me % 2
    partner = chip * 2 + 1 - core
    count = tok_ref.shape[0]
    _, row_parts, column_parts, _, _, columns = conv_full.shape
    depth = conv_full.shape[4]

    def peer_of(step):
        return (chip + step) % chips * 2 + core

    barrier = pltpu.get_barrier_semaphore()
    pl.semaphore_signal(barrier, inc=1, device_id=(partner, place), device_id_type=MESH)
    for step in range(1, chips):
        pl.semaphore_signal(
            barrier, inc=1, device_id=(peer_of(step), place), device_id_type=MESH
        )
    for turn in range(1, members):
        pl.semaphore_signal(
            barrier, inc=1, device_id=(me, (place + turn) % members), device_id_type=MESH
        )
    pl.semaphore_wait(barrier, 1 + (chips - 1) + (members - 1))

    right = (place + 1) % members
    left = (place + members - 1) % members
    halo = [
        pltpu.make_async_remote_copy(
            tok_ref.at[count - 8 : count], low_ref, halo_send.at[0], halo_recv.at[0], (me, right), MESH
        ),
        pltpu.make_async_remote_copy(
            tok_ref.at[0:8], high_ref, halo_send.at[1], halo_recv.at[1], (me, left), MESH
        ),
    ]
    for copy in halo:
        copy.start()

    def conv_source(spot):
        rows = pl.multiple_of(spot // column_parts * depth, depth)
        at = pl.multiple_of(spot % column_parts * columns, columns)
        return conv_ref.at[:, pl.ds(rows, depth), pl.ds(at, columns)]

    def conv_slot(way, spot):
        return conv_full.at[way, spot // column_parts, spot % column_parts]

    def attn_source(spot):
        return attn_ref.at[spot]

    def attn_slot(way, spot):
        return attn_full.at[way, spot]

    def conv_half(way, spot, half, turn):
        cut = columns // 256 * 128
        where = pl.ds(0, cut) if half == 0 else pl.ds(cut, columns - cut)
        return conv_full.at[way, spot // column_parts, spot % column_parts, :, :, where]

    def attn_half(way, spot, half, turn):
        rows = attn_ref.shape[1]
        tiles = rows // 16
        cut = (tiles // 2 if turn % 2 else tiles - tiles // 2) * 16
        where = pl.ds(0, cut) if half == 0 else pl.ds(cut, rows - cut)
        return attn_full.at[way, spot, where]

    kinds = ((conv_source, conv_slot, conv_half), (attn_source, attn_slot, attn_half))
    along_x = place + 1 - 2 * (place % 2)
    along_y = place + 2 - 4 * (place // 2)
    across = 3 - place
    sent = ([], [])
    local = ([], [])

    def send(kind, source, way, spot, target):
        copy = pltpu.make_async_remote_copy(
            source,
            kinds[kind][1](way, spot),
            send_sem.at[kind, len(sent[kind])],
            recv_sem.at[kind, way, spot],
            target,
            MESH,
        )
        copy.start()
        sent[kind].append(copy)

    def arrived(kind, way, spot):
        slot = kinds[kind][1](way, spot)
        pltpu.make_async_remote_copy(
            slot, slot, send_sem.at[kind, 0], recv_sem.at[kind, way, spot], (partner, place), MESH
        ).wait_recv()

    def first(kind):
        source, slot, _ = kinds[kind]
        for step in range(1, chips):
            send(kind, source(place), me, place, (peer_of(step), place))
        for spot in range(members):
            send(kind, source(spot), me, spot, (partner, place))
            copy = pltpu.make_async_copy(source(spot), slot(me, spot), local_sem.at[kind, spot])
            copy.start()
            local[kind].append(copy)

    order = sorted(range(1, chips), key=lambda step: min(step, chips - step))

    def second(kind, some):
        slot = kinds[kind][1]
        for step in some:
            way = peer_of(step)
            arrived(kind, way, place)
            send(kind, slot(way, place), way, place, (me, along_x))
            send(kind, slot(way, place), way, place, (me, along_y))
            send(kind, slot(way, place), way, place, (partner, place))

    def send_half(kind, way, spot, half, turn, target):
        ref = kinds[kind][2](way, spot, half, turn)
        copy = pltpu.make_async_remote_copy(
            ref,
            ref,
            send_sem.at[kind, len(sent[kind])],
            half_sem.at[kind, way, half],
            (me, target),
            MESH,
        )
        copy.start()
        sent[kind].append(copy)

    def third(kind):
        slot = kinds[kind][1]
        for turn, step in enumerate(order):
            way = peer_of(step)
            arrived(kind, way, along_x)
            send_half(kind, way, along_x, 0, turn, along_y)
            send(kind, slot(way, along_x), way, along_x, (partner, place))
            arrived(kind, way, along_y)
            send_half(kind, way, along_y, 1, turn, along_x)
            send(kind, slot(way, along_y), way, along_y, (partner, place))

    def fourth(kind):
        slot, half_of = kinds[kind][1:]
        for turn, step in enumerate(order):
            way = peer_of(step)
            for half in range(2):
                ref = half_of(way, across, half, turn)
                pltpu.make_async_remote_copy(
                    ref, ref, send_sem.at[kind, 0], half_sem.at[kind, way, half], (partner, place), MESH
                ).wait_recv()
            send(kind, slot(way, across), way, across, (partner, place))

    def finish(kind):
        for step in range(chips):
            way = (chip + step) % chips * 2 + 1 - core
            for spot in range(members):
                arrived(kind, way, spot)
        for copy in local[kind]:
            copy.wait()
        for copy in sent[kind]:
            copy.wait_send()

    first(0)
    for copy in halo:
        copy.wait()
    low = jnp.where(place > 0, low_ref[7:8], 0)
    high = jnp.where(place < members - 1, high_ref[0:1], 0)
    stem_compute(
        tok_ref,
        low,
        high,
        stem_weight_ref,
        stem_bias_ref,
        gain_ref,
        ext_ref,
        text_ref,
        hot_ref,
        shifted_ref,
        rows_ref,
        lambda: second(0, order[:1]),
    )
    second(0, order[1:])
    first(1)
    third(0)
    second(1, order[:1])
    fourth(0)
    second(1, order[1:])
    finish(0)

    width = 256
    steps = columns // width
    group = 4
    channels = ext_ref.shape[1]
    big = jnp.full((count, width), jnp.finfo(jnp.float32).max, jnp.float32)

    def panel(index, nothing):
        b = index // steps
        inner = pl.multiple_of(index % steps * width, width)

        def block(m, carry):
            most, least = carry
            total = None
            for tap in range(KW):
                start = pl.multiple_of((m * group + tap) * count, count)
                part = jnp.dot(
                    ext_ref[pl.ds(start, group * count), :],
                    conv_full[:, :, b, tap, :, pl.ds(inner, width)].reshape(channels, width),
                    preferred_element_type=jnp.float32,
                )
                total = part if total is None else total + part
            for piece_index in range(group):
                piece = total[piece_index * count : (piece_index + 1) * count]
                most = jnp.maximum(most, piece)
                least = jnp.minimum(least, piece)
            return most, least

        most, least = lax.fori_loop(0, POOL_B // group, block, (-big, big))
        at = pl.multiple_of(index * width, width)
        bias = conv_bias_ref[:, pl.ds(at, width)]
        coarse_ref[:, pl.ds(at, width)] = jnp.maximum(
            jax.nn.gelu(most + bias), jax.nn.gelu(least + bias)
        ).astype(jnp.bfloat16)
        return nothing

    panels = column_parts * steps
    early = panels // 2
    lax.fori_loop(0, early, panel, 0)
    third(1)
    lax.fori_loop(early, panels, panel, 0)
    fourth(1)
    finish(1)
    split = HEADS * HEAD_K
    middle = split + HEAD_K

    def weight(begin, end):
        return attn_full[:, :, :, begin:end].reshape(wide, end - begin)

    def turned(head):
        return (
            head * cosine_ref[...] + pltpu.roll(head, HEAD_K // 2, 1) * sine_ref[...]
        ).astype(jnp.bfloat16)

    hidden = rms_scale(coarse_ref[...].astype(jnp.float32), attn_gain_ref[...]).astype(
        jnp.bfloat16
    )
    key_ref[place] = turned(
        jnp.dot(hidden, weight(split, middle), preferred_element_type=jnp.float32)
    )
    value_ref[place] = jnp.dot(
        hidden, weight(middle + wide, middle + wide + HEAD_V), preferred_element_type=jnp.float32
    ).astype(jnp.bfloat16)
    pairs = []
    for turn in range(1, members):
        for index, ref in enumerate((key_ref, value_ref)):
            copy = pltpu.make_async_remote_copy(
                ref.at[place],
                ref.at[place],
                pair_send.at[index, turn],
                pair_recv.at[index, place],
                (me, (place + turn) % members),
                MESH,
            )
            copy.start()
            pairs.append(copy)
    query = jnp.dot(hidden, weight(0, split), preferred_element_type=jnp.float32)
    for turn in range(1, members):
        spot = (place + turn) % members
        for index, ref in enumerate((key_ref, value_ref)):
            pltpu.make_async_remote_copy(
                ref.at[spot],
                ref.at[spot],
                pair_send.at[index, 0],
                pair_recv.at[index, spot],
                (partner, place),
                MESH,
            ).wait_recv()
    keys = key_ref[...].reshape(members * count, HEAD_K)
    values = value_ref[...].reshape(members * count, HEAD_V)
    projection = weight(middle, middle + wide)
    total = coarse_ref[...].astype(jnp.float32)
    for head in range(HEADS):
        scores = lax.dot_general(
            turned(query[:, head * HEAD_K : (head + 1) * HEAD_K]),
            keys,
            (((1,), (1,)), ((), ())),
            preferred_element_type=jnp.float32,
        ) * HEAD_K ** (-0.5)
        raised = jnp.exp(scores - jnp.max(scores, axis=-1, keepdims=True))
        weights = (raised / jnp.sum(raised, axis=-1, keepdims=True)).astype(jnp.bfloat16)
        mixed = jnp.dot(weights, values, preferred_element_type=jnp.float32).astype(jnp.bfloat16)
        total = total + jnp.dot(
            mixed,
            projection[head * HEAD_V : (head + 1) * HEAD_V],
            preferred_element_type=jnp.float32,
        )
    out_ref[...] = total.astype(jnp.bfloat16)
    for copy in pairs:
        copy.wait_send()


def row_parts_of(depth, columns, members):
    for row_parts in (2, 1, 3):
        column_parts = members // row_parts
        if members % row_parts or depth % (16 * row_parts) or columns % (256 * column_parts):
            continue
        return row_parts, column_parts
    return None


def encoder_stage(tokens, stem_weight, vectors, cosine, sine, conv_weight, attn_rows, parts):
    count = tokens.shape[0]
    channels = stem_weight.shape[1]
    taps, depth, columns = conv_weight.shape
    ways = lax.axis_size("dp")
    members = lax.axis_size("seq")
    row_parts, column_parts = parts
    copies = (ways // 2 - 1) * (2 * members) + members + ways
    full_attn = (ways,) + attn_rows.shape
    vmem = pl.BlockSpec(memory_space=pltpu.VMEM)
    hbm = pl.BlockSpec(memory_space=pl.ANY)
    return pl.pallas_call(
        encoder_kernel,
        out_shape=jax.ShapeDtypeStruct((count, columns), jnp.bfloat16),
        in_specs=[vmem] * 5 + [hbm] * 2,
        out_specs=vmem,
        scratch_shapes=[
            pltpu.VMEM((count, columns), jnp.bfloat16),
            pltpu.VMEM((members, count, HEAD_K), jnp.bfloat16),
            pltpu.VMEM((members, count, HEAD_V), jnp.bfloat16),
            pltpu.SemaphoreType.DMA((2, members)),
            pltpu.SemaphoreType.DMA((2, members)),
            pltpu.VMEM((GROUP + 2 * SPAN, count), jnp.float32),
            pltpu.VMEM((POOL_B + 1, count, GROUP), jnp.bfloat16),
            pltpu.VMEM((POOL_A, GROUP, channels), jnp.bfloat16),
            pltpu.VMEM((count, channels), jnp.float32),
            pltpu.VMEM(((POOL_B + 4) * count, channels), jnp.bfloat16),
            pltpu.VMEM((8, GROUP), jnp.int32),
            pltpu.VMEM((8, GROUP), jnp.int32),
            pltpu.VMEM(
                (ways, row_parts, column_parts, taps, depth // row_parts, columns // column_parts),
                jnp.bfloat16,
            ),
            pltpu.VMEM(full_attn, jnp.bfloat16),
            pltpu.SemaphoreType.DMA((2,)),
            pltpu.SemaphoreType.DMA((2,)),
            pltpu.SemaphoreType.DMA((2, copies)),
            pltpu.SemaphoreType.DMA((2, ways, members)),
            pltpu.SemaphoreType.DMA((2, ways, 2)),
            pltpu.SemaphoreType.DMA((2, members)),
        ],
        compiler_params=pltpu.CompilerParams(
            collective_id=0, has_side_effects=True, vmem_limit_bytes=56 * 2**20
        ),
        name="encoder_stage",
    )(tokens, stem_weight, vectors[None], cosine, sine, conv_weight, attn_rows)


def gather_conv(conv_weight):
    taps, depth, columns = conv_weight.shape
    members = lax.axis_size("seq")
    place = lax.axis_index("seq")
    for row_parts in (2, 1, 3):
        column_parts = members // row_parts
        if members % row_parts or depth % (16 * row_parts) or columns % (256 * column_parts):
            continue
        depth_part = depth // row_parts
        column_part = columns // column_parts
        piece = lax.dynamic_slice(
            conv_weight,
            (0, place // column_parts * depth_part, place % column_parts * column_part),
            (taps, depth_part, column_part),
        )
        full = lax.all_gather(piece, ("dp", "seq"), axis=0, tiled=False)
        return full.reshape(-1, row_parts, column_parts, taps, depth_part, column_part)
    full = lax.all_gather(conv_weight, "dp", axis=0, tiled=False)
    return full[:, None, None]


def gather_rows(weight):
    members = lax.axis_size("seq")
    rows = weight.shape[0] // members
    piece = lax.dynamic_slice_in_dim(weight, lax.axis_index("seq") * rows, rows, axis=0)
    return lax.all_gather(piece, ("dp", "seq"), axis=0, tiled=True)


def body(
    tokens,
    stem_weight,
    stem_bias,
    conv_gain,
    conv_weight,
    conv_bias,
    attn_gain,
    w_query,
    w_key,
    w_value,
    w_out,
):
    seq_local = tokens.shape[1]
    rows_att = seq_local // GROUP
    tokens = tokens.reshape(rows_att, GROUP)
    size = lax.axis_size("seq")
    rows = w_out.shape[0]
    parts = row_parts_of(conv_weight.shape[1], conv_weight.shape[2], size)
    split = HEADS * HEAD_K
    if size == 4 and parts is not None and rows % (16 * size) == 0:
        packed = jnp.concatenate([w_query, w_key, w_out, w_value], axis=1)
        half_dim = HEAD_K // 2
        freqs = 10000.0 ** (-jnp.arange(half_dim, dtype=jnp.float32) / half_dim)
        positions = lax.axis_index("seq") * rows_att + jnp.arange(rows_att, dtype=jnp.int32)
        angles = positions.astype(jnp.float32)[:, None] * freqs[None, :]
        cosine, sine = jnp.cos(angles), jnp.sin(angles)
        return encoder_stage(
            tokens,
            stem_weight,
            jnp.concatenate([stem_bias, conv_gain, conv_bias, attn_gain]),
            jnp.concatenate([cosine, cosine], axis=1),
            jnp.concatenate([-sine, sine], axis=1),
            conv_weight,
            packed.reshape(size, rows // size, -1),
            parts,
        )[None]
    else:
        full_conv = gather_conv(conv_weight)
        projections = gather_rows(jnp.concatenate([w_query, w_key, w_value], axis=1))
        first_rows = projections[:, : split + HEAD_K]
        value_rows = projections[:, split + HEAD_K :]
        full_out = gather_rows(w_out)
        forward = [(i, i + 1) for i in range(size - 1)]
        backward = [(i + 1, i) for i in range(size - 1)]
        low = lax.ppermute(tokens[-1:], "seq", forward)
        high = lax.ppermute(tokens[:1], "seq", backward)
        ext = stem_stage(tokens, low, high, stem_weight, stem_bias, conv_gain)
        coarse = conv_stage(ext, full_conv, conv_bias)
    residual = coarse.astype(jnp.float32)
    hidden = rms_scale(residual, attn_gain).astype(jnp.bfloat16)
    projected = jnp.dot(hidden, first_rows, preferred_element_type=jnp.float32)
    query = projected[:, :split]
    keys = projected[:, split:]
    values = jnp.dot(hidden, value_rows, preferred_element_type=jnp.float32)
    half_dim = HEAD_K // 2
    freqs = 10000.0 ** (-jnp.arange(half_dim, dtype=jnp.float32) / half_dim)
    positions = lax.axis_index("seq") * rows_att + jnp.arange(rows_att, dtype=jnp.int32)
    angles = positions.astype(jnp.float32)[:, None] * freqs[None, :]
    query = rotate(query.reshape(rows_att, HEADS, HEAD_K), angles[:, None, :]).astype(jnp.bfloat16)
    keys = rotate(keys, angles).astype(jnp.bfloat16)
    pair = jnp.concatenate([keys, values.astype(jnp.bfloat16)], axis=1)
    pair = lax.all_gather(pair, "seq", axis=0, tiled=True)
    keys_all, values_all = pair[:, :HEAD_K], pair[:, HEAD_K:]
    scores = jnp.einsum(
        "rhd,kd->hrk", query, keys_all, preferred_element_type=jnp.float32
    ) * HEAD_K ** (-0.5)
    weights = jax.nn.softmax(scores, axis=-1).astype(jnp.bfloat16)
    mixed = jnp.einsum(
        "hrk,kd->rhd", weights, values_all, preferred_element_type=jnp.float32
    ).astype(jnp.bfloat16)
    mixed = mixed.reshape(rows_att, HEADS * HEAD_V)
    out = jnp.dot(mixed, full_out, preferred_element_type=jnp.float32)
    return (residual + out).astype(jnp.bfloat16)[None]


def solution(mesh):
    in_specs = (
        P("dp", "seq"),
        P(),
        P(),
        P(),
        P(None, "dp", None),
        P(),
        P(),
        P("dp", None),
        P("dp", None),
        P("dp", None),
        P("dp", None),
    )
    out_specs = P("dp", "seq", None)
    return jax.shard_map(body, mesh=mesh, in_specs=in_specs, out_specs=out_specs, check_vma=False)
```

```python
import functools

import jax
import jax.numpy as jnp
from jax import lax
from jax.experimental import pallas as pl
from jax.experimental.pallas import tpu as pltpu
from jax.sharding import PartitionSpec as P

HEADS = 8
HEAD_K = 128
HEAD_V = 192
KW_STEM = 15
KW = 5
POOL_A = 8
POOL_B = 16
GROUP = POOL_A * POOL_B
SPAN = 24

epsilon = 1e-06


def rms_scale(values, gain):
    return values * lax.rsqrt(jnp.mean(values * values, axis=-1, keepdims=True) + epsilon) * gain


def rotate(values, angles):
    half_dim = values.shape[-1] // 2
    first = values[..., :half_dim]
    second = values[..., half_dim:]
    cosine = jnp.cos(angles)
    sine = jnp.sin(angles)
    return jnp.concatenate(
        [first * cosine - second * sine, second * cosine + first * sine], axis=-1
    )


def stem_kernel(
    tok_ref, low_ref, high_ref, weight_ref, bias_ref, gain_ref, ext_ref, text_ref, hot_ref, shifted_ref, rows_ref
):
    stem_compute(
        tok_ref,
        low_ref[...],
        high_ref[...],
        weight_ref,
        bias_ref,
        gain_ref,
        ext_ref,
        text_ref,
        hot_ref,
        shifted_ref,
        rows_ref,
    )


def stem_compute(
    tok_ref, low, high, weight_ref, bias_ref, gain_ref, ext_ref, text_ref, hot_ref, shifted_ref, rows_ref, between=None
):
    count = tok_ref.shape[0]
    channels = weight_ref.shape[1]
    place = lax.axis_index("seq")
    last_place = lax.axis_size("seq") - 1
    main = tok_ref[...].astype(jnp.float32)
    row = lax.broadcasted_iota(jnp.int32, main.shape, 0)
    previous = jnp.where(row == 0, low.astype(jnp.float32), pltpu.roll(main, 1, 0))
    following = jnp.where(
        row == count - 1, high.astype(jnp.float32), pltpu.roll(main, count - 1, 0)
    )
    text_ref[0:SPAN, :] = previous.T[GROUP - SPAN :, :]
    text_ref[SPAN : SPAN + GROUP, :] = main.T
    text_ref[SPAN + GROUP :, :] = following.T[:SPAN, :]

    source = lax.broadcasted_iota(jnp.int32, (GROUP, weight_ref.shape[0]), 1)
    target = lax.broadcasted_iota(jnp.int32, (GROUP, weight_ref.shape[0]), 0)
    tap = source // 4
    base = source - 4 * tap
    for offset in range(POOL_A):
        pick = (target == base * SPAN + offset + tap + 1).astype(jnp.float32).astype(jnp.bfloat16)
        shifted_ref[offset] = jnp.dot(
            pick, weight_ref[...], preferred_element_type=jnp.float32
        ).astype(jnp.bfloat16)

    def hot_of(span):
        planes = [(span == float(code)).astype(jnp.float32) for code in range(1, 5)]
        planes.append(jnp.zeros((GROUP - 4 * SPAN, span.shape[1]), jnp.float32))
        return jnp.concatenate(planes, axis=0).T.astype(jnp.bfloat16)

    for j in range(POOL_B):
        hot_ref[j] = hot_of(text_ref[8 * j + SPAN - 8 : 8 * j + 2 * SPAN - 8, :])
    lane = lax.broadcasted_iota(jnp.int32, (SPAN, count), 1)
    edge = jnp.where(
        lane == 0,
        text_ref[0:SPAN, :],
        jnp.where(
            lane == 1,
            pltpu.roll(text_ref[8 : 8 + SPAN, :], 1, 1),
            jnp.where(
                lane == 2,
                pltpu.roll(text_ref[GROUP + SPAN - 8 : GROUP + 2 * SPAN - 8, :], 3, 1),
                pltpu.roll(text_ref[GROUP + SPAN : GROUP + 2 * SPAN, :], 4, 1),
            ),
        ),
    )
    hot_ref[POOL_B] = hot_of(edge)

    width = 256

    def block(j, carry):
        hot = hot_ref[j]
        for chunk in range(channels // width):
            columns = slice(chunk * width, (chunk + 1) * width)
            best = None
            for offset in range(POOL_A):
                stem = jnp.dot(
                    hot, shifted_ref[offset, :, columns], preferred_element_type=jnp.float32
                )
                best = stem if best is None else jnp.maximum(best, stem)
            pooled = jax.nn.gelu(best + bias_ref[:, columns]).astype(jnp.bfloat16)
            rows_ref[:, columns] = pooled.astype(jnp.float32)
        pooled = rows_ref[...]
        start = pl.multiple_of((j + 2) * count, count)
        ext_ref[pl.ds(start, count), :] = rms_scale(pooled, gain_ref[...]).astype(jnp.bfloat16)
        return carry

    if between is None:
        lax.fori_loop(0, POOL_B + 1, block, 0)
    else:
        lax.fori_loop(0, POOL_B // 2, block, 0)
        between()
        lax.fori_loop(POOL_B // 2, POOL_B + 1, block, 0)
    edges = ext_ref[(POOL_B + 2) * count : (POOL_B + 3) * count, :].astype(jnp.float32)
    left_keep = (place > 0).astype(jnp.float32)
    right_keep = (place < last_place).astype(jnp.float32)
    spot = lax.broadcasted_iota(jnp.int32, (count, channels), 0)
    for index in range(2):
        inner = ext_ref[(POOL_B + index) * count : (POOL_B + index + 1) * count, :]
        moved = pltpu.roll(inner.astype(jnp.float32), 1, 0)
        ext_ref[index * count : (index + 1) * count, :] = jnp.where(
            spot == 0, edges[index : index + 1, :] * left_keep, moved
        ).astype(jnp.bfloat16)
        inner = ext_ref[(2 + index) * count : (3 + index) * count, :]
        moved = pltpu.roll(inner.astype(jnp.float32), count - 1, 0)
        at = POOL_B + 2 + index
        ext_ref[at * count : (at + 1) * count, :] = jnp.where(
            spot == count - 1, edges[2 + index : 3 + index, :] * right_keep, moved
        ).astype(jnp.bfloat16)


def stem_stage(tokens, low, high, stem_weight, stem_bias, conv_gain):
    count = tokens.shape[0]
    channels = stem_weight.shape[1]
    return pl.pallas_call(
        stem_kernel,
        out_shape=jax.ShapeDtypeStruct(((POOL_B + 4) * count, channels), jnp.bfloat16),
        in_specs=[pl.BlockSpec(memory_space=pltpu.VMEM)] * 6,
        out_specs=pl.BlockSpec(memory_space=pltpu.VMEM),
        scratch_shapes=[
            pltpu.VMEM((GROUP + 2 * SPAN, count), jnp.float32),
            pltpu.VMEM((POOL_B + 1, count, GROUP), jnp.bfloat16),
            pltpu.VMEM((POOL_A, GROUP, channels), jnp.bfloat16),
            pltpu.VMEM((count, channels), jnp.float32),
        ],
        cost_estimate=pl.CostEstimate(
            flops=20_000_000_000, bytes_accessed=4_000_000, transcendentals=1_600_000
        ),
        name="stem_stage",
    )(tokens, low, high, stem_weight, stem_bias[None], conv_gain[None])


def conv_kernel(count, ext_ref, weight_ref, bias_ref, coarse_ref):
    group = 4
    width = weight_ref.shape[-1]
    channels = ext_ref.shape[1]

    def block(m, carry):
        most, least = carry
        total = None
        for tap in range(KW):
            start = pl.multiple_of((m * group + tap) * count, count)
            part = jnp.dot(
                ext_ref[pl.ds(start, group * count), :],
                weight_ref[:, :, 0, tap].reshape(channels, width),
                preferred_element_type=jnp.float32,
            )
            total = part if total is None else total + part
        for index in range(group):
            piece = total[index * count : (index + 1) * count]
            most = jnp.maximum(most, piece)
            least = jnp.minimum(least, piece)
        return most, least

    big = jnp.full((count, width), jnp.finfo(jnp.float32).max, jnp.float32)
    most, least = lax.fori_loop(0, POOL_B // group, block, (-big, big))
    bias = bias_ref[...]
    coarse_ref[...] = jnp.maximum(jax.nn.gelu(most + bias), jax.nn.gelu(least + bias)).astype(
        jnp.bfloat16
    )


def conv_stage(ext, weight, conv_bias):
    count = ext.shape[0] // (POOL_B + 4)
    ways, row_parts, column_parts, taps, depth, columns = weight.shape
    width = 256
    steps = columns // width
    return pl.pallas_call(
        functools.partial(conv_kernel, count),
        grid=(column_parts, steps),
        out_shape=jax.ShapeDtypeStruct((count, column_parts * columns), jnp.bfloat16),
        in_specs=[
            pl.BlockSpec(ext.shape, lambda b, n: (0, 0), pipeline_mode=pl.Buffered(1)),
            pl.BlockSpec(
                (ways, row_parts, 1, taps, depth, width), lambda b, n: (0, 0, b, 0, 0, n)
            ),
            pl.BlockSpec((1, width), lambda b, n: (0, b * steps + n)),
        ],
        out_specs=pl.BlockSpec((count, width), lambda b, n: (0, b * steps + n)),
        cost_estimate=pl.CostEstimate(
            flops=24_000_000_000, bytes_accessed=16_000_000, transcendentals=400_000
        ),
        name="conv_stage",
    )(ext, weight, conv_bias[None])


MESH = pl.DeviceIdType.MESH


def encoder_kernel(
    tok_ref,
    stem_weight_ref,
    vector_ref,
    cosine_ref,
    sine_ref,
    conv_ref,
    attn_ref,
    out_ref,
    coarse_ref,
    key_ref,
    value_ref,
    pair_send,
    pair_recv,
    text_ref,
    hot_ref,
    shifted_ref,
    rows_ref,
    ext_ref,
    low_ref,
    high_ref,
    conv_full,
    attn_full,
    halo_send,
    halo_recv,
    send_sem,
    recv_sem,
    half_sem,
    local_sem,
):
    stem_wide = stem_weight_ref.shape[1]
    wide = out_ref.shape[1]
    stem_bias_ref = vector_ref.at[:, 0:stem_wide]
    gain_ref = vector_ref.at[:, stem_wide : 2 * stem_wide]
    conv_bias_ref = vector_ref.at[:, 2 * stem_wide : 2 * stem_wide + wide]
    attn_gain_ref = vector_ref.at[:, 2 * stem_wide + wide :]
    ways = lax.axis_size("dp")
    members = lax.axis_size("seq")
    chips = ways // 2
    me = lax.axis_index("dp")
    place = lax.axis_index("seq")
    chip = me // 2
    core = me % 2
    partner = chip * 2 + 1 - core
    count = tok_ref.shape[0]
    _, row_parts, column_parts, _, _, columns = conv_full.shape
    depth = conv_full.shape[4]

    def peer_of(step):
        return (chip + step) % chips * 2 + core

    barrier = pltpu.get_barrier_semaphore()
    pl.semaphore_signal(barrier, inc=1, device_id=(partner, place), device_id_type=MESH)
    for step in range(1, chips):
        pl.semaphore_signal(
            barrier, inc=1, device_id=(peer_of(step), place), device_id_type=MESH
        )
    for turn in range(1, members):
        pl.semaphore_signal(
            barrier, inc=1, device_id=(me, (place + turn) % members), device_id_type=MESH
        )
    pl.semaphore_wait(barrier, 1 + (chips - 1) + (members - 1))

    right = (place + 1) % members
    left = (place + members - 1) % members
    halo = [
        pltpu.make_async_remote_copy(
            tok_ref.at[count - 8 : count], low_ref, halo_send.at[0], halo_recv.at[0], (me, right), MESH
        ),
        pltpu.make_async_remote_copy(
            tok_ref.at[0:8], high_ref, halo_send.at[1], halo_recv.at[1], (me, left), MESH
        ),
    ]
    for copy in halo:
        copy.start()

    def conv_source(spot):
        rows = pl.multiple_of(spot // column_parts * depth, depth)
        at = pl.multiple_of(spot % column_parts * columns, columns)
        return conv_ref.at[:, pl.ds(rows, depth), pl.ds(at, columns)]

    def conv_slot(way, spot):
        return conv_full.at[way, spot // column_parts, spot % column_parts]

    def attn_source(spot):
        return attn_ref.at[spot]

    def attn_slot(way, spot):
        return attn_full.at[way, spot]

    def conv_half(way, spot, half, turn):
        cut = columns // 256 * 128
        where = pl.ds(0, cut) if half == 0 else pl.ds(cut, columns - cut)
        return conv_full.at[way, spot // column_parts, spot % column_parts, :, :, where]

    def attn_half(way, spot, half, turn):
        rows = attn_ref.shape[1]
        tiles = rows // 16
        cut = (tiles // 2 if turn % 2 else tiles - tiles // 2) * 16
        where = pl.ds(0, cut) if half == 0 else pl.ds(cut, rows - cut)
        return attn_full.at[way, spot, where]

    kinds = ((conv_source, conv_slot, conv_half), (attn_source, attn_slot, attn_half))
    along_x = place + 1 - 2 * (place % 2)
    along_y = place + 2 - 4 * (place // 2)
    across = 3 - place
    sent = ([], [])
    local = ([], [])

    def send(kind, source, way, spot, target):
        copy = pltpu.make_async_remote_copy(
            source,
            kinds[kind][1](way, spot),
            send_sem.at[kind, len(sent[kind])],
            recv_sem.at[kind, way, spot],
            target,
            MESH,
        )
        copy.start()
        sent[kind].append(copy)

    def arrived(kind, way, spot):
        slot = kinds[kind][1](way, spot)
        pltpu.make_async_remote_copy(
            slot, slot, send_sem.at[kind, 0], recv_sem.at[kind, way, spot], (partner, place), MESH
        ).wait_recv()

    def first(kind):
        source, slot, _ = kinds[kind]
        for step in range(1, chips):
            send(kind, source(place), me, place, (peer_of(step), place))
        for spot in range(members):
            send(kind, source(spot), me, spot, (partner, place))
            copy = pltpu.make_async_copy(source(spot), slot(me, spot), local_sem.at[kind, spot])
            copy.start()
            local[kind].append(copy)

    order = sorted(range(1, chips), key=lambda step: min(step, chips - step))

    def second(kind, some):
        slot = kinds[kind][1]
        for step in some:
            way = peer_of(step)
            arrived(kind, way, place)
            send(kind, slot(way, place), way, place, (me, along_x))
            send(kind, slot(way, place), way, place, (me, along_y))
            send(kind, slot(way, place), way, place, (partner, place))

    def send_half(kind, way, spot, half, turn, target):
        ref = kinds[kind][2](way, spot, half, turn)
        copy = pltpu.make_async_remote_copy(
            ref,
            ref,
            send_sem.at[kind, len(sent[kind])],
            half_sem.at[kind, way, half],
            (me, target),
            MESH,
        )
        copy.start()
        sent[kind].append(copy)

    def third(kind):
        slot = kinds[kind][1]
        for turn, step in enumerate(order):
            way = peer_of(step)
            arrived(kind, way, along_x)
            send_half(kind, way, along_x, 0, turn, along_y)
            send(kind, slot(way, along_x), way, along_x, (partner, place))
            arrived(kind, way, along_y)
            send_half(kind, way, along_y, 1, turn, along_x)
            send(kind, slot(way, along_y), way, along_y, (partner, place))

    def fourth(kind):
        slot, half_of = kinds[kind][1:]
        for turn, step in enumerate(order):
            way = peer_of(step)
            for half in range(2):
                ref = half_of(way, across, half, turn)
                pltpu.make_async_remote_copy(
                    ref, ref, send_sem.at[kind, 0], half_sem.at[kind, way, half], (partner, place), MESH
                ).wait_recv()
            send(kind, slot(way, across), way, across, (partner, place))

    def finish(kind):
        for step in range(chips):
            way = (chip + step) % chips * 2 + 1 - core
            for spot in range(members):
                arrived(kind, way, spot)
        for copy in local[kind]:
            copy.wait()
        for copy in sent[kind]:
            copy.wait_send()

    first(0)
    for copy in halo:
        copy.wait()
    low = jnp.where(place > 0, low_ref[7:8], 0)
    high = jnp.where(place < members - 1, high_ref[0:1], 0)
    stem_compute(
        tok_ref,
        low,
        high,
        stem_weight_ref,
        stem_bias_ref,
        gain_ref,
        ext_ref,
        text_ref,
        hot_ref,
        shifted_ref,
        rows_ref,
        lambda: second(0, order[:1]),
    )
    second(0, order[1:])
    first(1)
    third(0)
    second(1, order[:1])
    fourth(0)
    second(1, order[1:])
    finish(0)

    width = 256
    steps = columns // width
    group = 8
    channels = ext_ref.shape[1]
    big = jnp.full((count, width), jnp.finfo(jnp.float32).max, jnp.float32)

    def panel(index, nothing):
        b = index // steps
        inner = pl.multiple_of(index % steps * width, width)

        def block(m, carry):
            most, least = carry
            total = None
            for tap in range(KW):
                start = pl.multiple_of((m * group + tap) * count, count)
                part = jnp.dot(
                    ext_ref[pl.ds(start, group * count), :],
                    conv_full[:, :, b, tap, :, pl.ds(inner, width)].reshape(channels, width),
                    preferred_element_type=jnp.float32,
                )
                total = part if total is None else total + part
            for piece_index in range(group):
                piece = total[piece_index * count : (piece_index + 1) * count]
                most = jnp.maximum(most, piece)
                least = jnp.minimum(least, piece)
            return most, least

        most, least = lax.fori_loop(0, POOL_B // group, block, (-big, big))
        at = pl.multiple_of(index * width, width)
        bias = conv_bias_ref[:, pl.ds(at, width)]
        coarse_ref[:, pl.ds(at, width)] = jnp.maximum(
            jax.nn.gelu(most + bias), jax.nn.gelu(least + bias)
        ).astype(jnp.bfloat16)
        return nothing

    panels = column_parts * steps
    early = panels // 2
    lax.fori_loop(0, early, panel, 0)
    third(1)
    lax.fori_loop(early, panels, panel, 0)
    fourth(1)
    finish(1)
    split = HEADS * HEAD_K
    middle = split + HEAD_K

    def weight(begin, end):
        return attn_full[:, :, :, begin:end].reshape(wide, end - begin)

    def turned(head):
        return (
            head * cosine_ref[...] + pltpu.roll(head, HEAD_K // 2, 1) * sine_ref[...]
        ).astype(jnp.bfloat16)

    hidden = rms_scale(coarse_ref[...].astype(jnp.float32), attn_gain_ref[...]).astype(
        jnp.bfloat16
    )
    key_ref[place] = turned(
        jnp.dot(hidden, weight(split, middle), preferred_element_type=jnp.float32)
    )
    value_ref[place] = jnp.dot(
        hidden, weight(middle + wide, middle + wide + HEAD_V), preferred_element_type=jnp.float32
    ).astype(jnp.bfloat16)
    pairs = []
    for turn in range(1, members):
        for index, ref in enumerate((key_ref, value_ref)):
            copy = pltpu.make_async_remote_copy(
                ref.at[place],
                ref.at[place],
                pair_send.at[index, turn],
                pair_recv.at[index, place],
                (me, (place + turn) % members),
                MESH,
            )
            copy.start()
            pairs.append(copy)
    query = jnp.dot(hidden, weight(0, split), preferred_element_type=jnp.float32)
    for turn in range(1, members):
        spot = (place + turn) % members
        for index, ref in enumerate((key_ref, value_ref)):
            pltpu.make_async_remote_copy(
                ref.at[spot],
                ref.at[spot],
                pair_send.at[index, 0],
                pair_recv.at[index, spot],
                (partner, place),
                MESH,
            ).wait_recv()
    keys = key_ref[...].reshape(members * count, HEAD_K)
    values = value_ref[...].reshape(members * count, HEAD_V)
    projection = weight(middle, middle + wide)
    total = coarse_ref[...].astype(jnp.float32)
    for head in range(HEADS):
        scores = lax.dot_general(
            turned(query[:, head * HEAD_K : (head + 1) * HEAD_K]),
            keys,
            (((1,), (1,)), ((), ())),
            preferred_element_type=jnp.float32,
        ) * HEAD_K ** (-0.5)
        raised = jnp.exp(scores - jnp.max(scores, axis=-1, keepdims=True))
        weights = (raised / jnp.sum(raised, axis=-1, keepdims=True)).astype(jnp.bfloat16)
        mixed = jnp.dot(weights, values, preferred_element_type=jnp.float32).astype(jnp.bfloat16)
        total = total + jnp.dot(
            mixed,
            projection[head * HEAD_V : (head + 1) * HEAD_V],
            preferred_element_type=jnp.float32,
        )
    out_ref[...] = total.astype(jnp.bfloat16)
    for copy in pairs:
        copy.wait_send()


def row_parts_of(depth, columns, members):
    for row_parts in (2, 1, 3):
        column_parts = members // row_parts
        if members % row_parts or depth % (16 * row_parts) or columns % (256 * column_parts):
            continue
        return row_parts, column_parts
    return None


def encoder_stage(tokens, stem_weight, vectors, cosine, sine, conv_weight, attn_rows, parts):
    count = tokens.shape[0]
    channels = stem_weight.shape[1]
    taps, depth, columns = conv_weight.shape
    ways = lax.axis_size("dp")
    members = lax.axis_size("seq")
    row_parts, column_parts = parts
    copies = (ways // 2 - 1) * (2 * members) + members + ways
    full_attn = (ways,) + attn_rows.shape
    vmem = pl.BlockSpec(memory_space=pltpu.VMEM)
    hbm = pl.BlockSpec(memory_space=pl.ANY)
    return pl.pallas_call(
        encoder_kernel,
        out_shape=jax.ShapeDtypeStruct((count, columns), jnp.bfloat16),
        in_specs=[vmem] * 5 + [hbm] * 2,
        out_specs=vmem,
        scratch_shapes=[
            pltpu.VMEM((count, columns), jnp.bfloat16),
            pltpu.VMEM((members, count, HEAD_K), jnp.bfloat16),
            pltpu.VMEM((members, count, HEAD_V), jnp.bfloat16),
            pltpu.SemaphoreType.DMA((2, members)),
            pltpu.SemaphoreType.DMA((2, members)),
            pltpu.VMEM((GROUP + 2 * SPAN, count), jnp.float32),
            pltpu.VMEM((POOL_B + 1, count, GROUP), jnp.bfloat16),
            pltpu.VMEM((POOL_A, GROUP, channels), jnp.bfloat16),
            pltpu.VMEM((count, channels), jnp.float32),
            pltpu.VMEM(((POOL_B + 4) * count, channels), jnp.bfloat16),
            pltpu.VMEM((8, GROUP), jnp.int32),
            pltpu.VMEM((8, GROUP), jnp.int32),
            pltpu.VMEM(
                (ways, row_parts, column_parts, taps, depth // row_parts, columns // column_parts),
                jnp.bfloat16,
            ),
            pltpu.VMEM(full_attn, jnp.bfloat16),
            pltpu.SemaphoreType.DMA((2,)),
            pltpu.SemaphoreType.DMA((2,)),
            pltpu.SemaphoreType.DMA((2, copies)),
            pltpu.SemaphoreType.DMA((2, ways, members)),
            pltpu.SemaphoreType.DMA((2, ways, 2)),
            pltpu.SemaphoreType.DMA((2, members)),
        ],
        compiler_params=pltpu.CompilerParams(
            collective_id=0, has_side_effects=True, vmem_limit_bytes=56 * 2**20
        ),
        name="encoder_stage",
    )(tokens, stem_weight, vectors[None], cosine, sine, conv_weight, attn_rows)


def gather_conv(conv_weight):
    taps, depth, columns = conv_weight.shape
    members = lax.axis_size("seq")
    place = lax.axis_index("seq")
    for row_parts in (2, 1, 3):
        column_parts = members // row_parts
        if members % row_parts or depth % (16 * row_parts) or columns % (256 * column_parts):
            continue
        depth_part = depth // row_parts
        column_part = columns // column_parts
        piece = lax.dynamic_slice(
            conv_weight,
            (0, place // column_parts * depth_part, place % column_parts * column_part),
            (taps, depth_part, column_part),
        )
        full = lax.all_gather(piece, ("dp", "seq"), axis=0, tiled=False)
        return full.reshape(-1, row_parts, column_parts, taps, depth_part, column_part)
    full = lax.all_gather(conv_weight, "dp", axis=0, tiled=False)
    return full[:, None, None]


def gather_rows(weight):
    members = lax.axis_size("seq")
    rows = weight.shape[0] // members
    piece = lax.dynamic_slice_in_dim(weight, lax.axis_index("seq") * rows, rows, axis=0)
    return lax.all_gather(piece, ("dp", "seq"), axis=0, tiled=True)


def body(
    tokens,
    stem_weight,
    stem_bias,
    conv_gain,
    conv_weight,
    conv_bias,
    attn_gain,
    w_query,
    w_key,
    w_value,
    w_out,
):
    seq_local = tokens.shape[1]
    rows_att = seq_local // GROUP
    tokens = tokens.reshape(rows_att, GROUP)
    size = lax.axis_size("seq")
    rows = w_out.shape[0]
    parts = row_parts_of(conv_weight.shape[1], conv_weight.shape[2], size)
    split = HEADS * HEAD_K
    if size == 4 and parts is not None and rows % (16 * size) == 0:
        packed = jnp.concatenate([w_query, w_key, w_out, w_value], axis=1)
        half_dim = HEAD_K // 2
        freqs = 10000.0 ** (-jnp.arange(half_dim, dtype=jnp.float32) / half_dim)
        positions = lax.axis_index("seq") * rows_att + jnp.arange(rows_att, dtype=jnp.int32)
        angles = positions.astype(jnp.float32)[:, None] * freqs[None, :]
        cosine, sine = jnp.cos(angles), jnp.sin(angles)
        return encoder_stage(
            tokens,
            stem_weight,
            jnp.concatenate([stem_bias, conv_gain, conv_bias, attn_gain]),
            jnp.concatenate([cosine, cosine], axis=1),
            jnp.concatenate([-sine, sine], axis=1),
            conv_weight,
            packed.reshape(size, rows // size, -1),
            parts,
        )[None]
    else:
        full_conv = gather_conv(conv_weight)
        projections = gather_rows(jnp.concatenate([w_query, w_key, w_value], axis=1))
        first_rows = projections[:, : split + HEAD_K]
        value_rows = projections[:, split + HEAD_K :]
        full_out = gather_rows(w_out)
        forward = [(i, i + 1) for i in range(size - 1)]
        backward = [(i + 1, i) for i in range(size - 1)]
        low = lax.ppermute(tokens[-1:], "seq", forward)
        high = lax.ppermute(tokens[:1], "seq", backward)
        ext = stem_stage(tokens, low, high, stem_weight, stem_bias, conv_gain)
        coarse = conv_stage(ext, full_conv, conv_bias)
    residual = coarse.astype(jnp.float32)
    hidden = rms_scale(residual, attn_gain).astype(jnp.bfloat16)
    projected = jnp.dot(hidden, first_rows, preferred_element_type=jnp.float32)
    query = projected[:, :split]
    keys = projected[:, split:]
    values = jnp.dot(hidden, value_rows, preferred_element_type=jnp.float32)
    half_dim = HEAD_K // 2
    freqs = 10000.0 ** (-jnp.arange(half_dim, dtype=jnp.float32) / half_dim)
    positions = lax.axis_index("seq") * rows_att + jnp.arange(rows_att, dtype=jnp.int32)
    angles = positions.astype(jnp.float32)[:, None] * freqs[None, :]
    query = rotate(query.reshape(rows_att, HEADS, HEAD_K), angles[:, None, :]).astype(jnp.bfloat16)
    keys = rotate(keys, angles).astype(jnp.bfloat16)
    pair = jnp.concatenate([keys, values.astype(jnp.bfloat16)], axis=1)
    pair = lax.all_gather(pair, "seq", axis=0, tiled=True)
    keys_all, values_all = pair[:, :HEAD_K], pair[:, HEAD_K:]
    scores = jnp.einsum(
        "rhd,kd->hrk", query, keys_all, preferred_element_type=jnp.float32
    ) * HEAD_K ** (-0.5)
    weights = jax.nn.softmax(scores, axis=-1).astype(jnp.bfloat16)
    mixed = jnp.einsum(
        "hrk,kd->rhd", weights, values_all, preferred_element_type=jnp.float32
    ).astype(jnp.bfloat16)
    mixed = mixed.reshape(rows_att, HEADS * HEAD_V)
    out = jnp.dot(mixed, full_out, preferred_element_type=jnp.float32)
    return (residual + out).astype(jnp.bfloat16)[None]


def solution(mesh):
    in_specs = (
        P("dp", "seq"),
        P(),
        P(),
        P(),
        P(None, "dp", None),
        P(),
        P(),
        P("dp", None),
        P("dp", None),
        P("dp", None),
        P("dp", None),
    )
    out_specs = P("dp", "seq", None)
    return jax.shard_map(body, mesh=mesh, in_specs=in_specs, out_specs=out_specs, check_vma=False)
```
